512 devices in a mesh: wide: 64 (over z, y_lo, x), narrow: 8 (over y_hi, core).
Axes of the slice: x: 4, y: 8 (y_hi: 4, y_lo: 2; y = y_hi * 2 + y_lo), z: 8, core: 2. Of those that a mesh axis runs over, the one named last changes fastest.
Arguments:
- activation_cache: bfloat16 [64, 128, 8192], P('wide', None, 'narrow'), may hold values from -6 to 6
- token_ids: int32 [64, 128], P('wide'), may hold values from 0 to 127
- cotangent: bfloat16 [64, 128, 37120], P('wide', None, 'narrow'), may hold values from -6 to 6
- adapter_b: float32 [64, 16, 8192], P('wide', None, 'narrow'), may hold values from -4 to 4
- first_b: float32 [64, 16, 8192], P('wide', None, 'narrow'), may hold values from -0.3 to 0.3
- second_b: float32 [64, 16, 8192], P('wide', None, 'narrow'), may hold values from 0.0001 to 0.002
- adapter_a: float32 [64, 16, 37120], P('wide', None, 'narrow'), may hold values from -4 to 4
- first_a: float32 [64, 16, 37120], P('wide', None, 'narrow'), may hold values from -0.3 to 0.3
- second_a: float32 [64, 16, 37120], P('wide', None, 'narrow'), may hold values from 0.0001 to 0.002
- resident: bfloat16 [8192, 37120], P('narrow', 'wide'), may hold values from -6 to 6
- block_owner: int32 [64], replicated, may hold values from 0 to 63, each once
- next_rows: bfloat16 [512, 8192], P('wide', 'narrow'), may hold values from -6 to 6
Outputs:
- merged: bfloat16 [8192, 37120], P('narrow', 'wide')
- projected: bfloat16 [512, 37120], P('narrow', 'wide')
The draws below stay inside these ranges and needn't reach their ends.
Inputs may be any that keep to these rules, and one draw needn't show every extreme that they name: `block_owner`: each column block is stored at exactly one position.
All inputs are finite; a program needn't handle non-finite values.
Results may differ from the reference program's by a relative error of at most 0.0058.
Values may be sent and summed in bfloat16 or wider, within the bound.
A program may use at most 64 MiB of HBM per device.

```python
import math
import jax
import jax.numpy as jnp
from jax import lax

D = 8192
FW = 37120
R = 16
WORKER_TOKENS = 128
POOL = 128
NEXT = 512
WORKER_COUNT = 64
NB = 64
FB = 580


def set_ends(entries, stream_key, least, top_value):
    dims = entries.shape
    spot = [jax.random.randint(jax.random.fold_in(stream_key, axis), (), 0, dims[axis]) for axis in range(len(dims))]
    entries = entries.at[tuple(spot)].set(least)
    longest = dims.index(max(dims))
    spot[longest] = (spot[longest] + 1) % dims[longest]
    return entries.at[tuple(spot)].set(top_value)


def block_levels(own_key, extent, cuts, smallest, high):
    gain, own = 1.0, jax.random.fold_in(own_key, 6)
    for axis_at, blocks in cuts:
        heights = jnp.exp(jax.random.uniform(jax.random.fold_in(own, axis_at), (blocks,), jnp.float32, smallest / len(cuts), high / len(cuts)))
        gain = gain * jnp.repeat(heights, extent[axis_at] // blocks).reshape([-1 if axis == axis_at else 1 for axis in range(len(extent))])
    return gain


def noise(key, shape, deviation, most, pieces=(), kind=jnp.bfloat16):
    factor_of = block_levels(key, shape, pieces, -0.22, 0.18) if pieces else 1.0
    result = jax.random.normal(key, shape, jnp.float32) * deviation * factor_of
    return jnp.minimum(jnp.maximum(result, -most), most).astype(kind)


def setup_inputs(seed: int = 0) -> dict:
    seeds = jax.random.split(jax.random.key(seed), 13)
    activation_cache = noise(seeds[0], (WORKER_COUNT, POOL, D), 1.0, 6.0, ((0, 64), (2, 8)))
    token_ids = set_ends(jax.random.randint(seeds[1], (WORKER_COUNT, WORKER_TOKENS), 0, POOL), jax.random.fold_in(seeds[1], 1), 0, POOL - 1).astype(jnp.int32)
    cotangent = noise(seeds[2], (WORKER_COUNT, WORKER_TOKENS, FW), 1.0, 6.0, ((0, 64), (2, 8)))
    adapter_b = noise(seeds[3], (WORKER_COUNT, R, D), 0.7, 4.0, ((0, 64), (2, 8)), jnp.float32)
    first_b = noise(seeds[4], (WORKER_COUNT, R, D), 0.05, 0.3, ((0, 64), (2, 8)), jnp.float32)
    second_b = jnp.clip(jnp.exp(math.log(0.002) - 2.9957323 * jax.random.uniform(seeds[5], (WORKER_COUNT, R, D), jnp.float32) ** block_levels(seeds[5], (WORKER_COUNT, R, D), ((0, 64), (2, 8)), -0.2, 0.2)), 0.0001, 0.002)
    adapter_a = noise(seeds[6], (WORKER_COUNT, R, FW), 0.7, 4.0, ((0, 64), (2, 8)), jnp.float32)
    first_a = noise(seeds[7], (WORKER_COUNT, R, FW), 0.05, 0.3, ((0, 64), (2, 8)), jnp.float32)
    second_a = jnp.clip(jnp.exp(math.log(0.002) - 2.9957323 * jax.random.uniform(seeds[8], (WORKER_COUNT, R, FW), jnp.float32) ** block_levels(seeds[8], (WORKER_COUNT, R, FW), ((0, 64), (2, 8)), -0.2, 0.2)), 0.0001, 0.002)
    resident = noise(seeds[9], (D, FW), 1.0, 6.0, ((0, 8), (1, 64)))
    block_owner = jax.random.permutation(seeds[10], NB).astype(jnp.int32)
    next_rows = noise(seeds[11], (NEXT, D), 1.0, 6.0, ((0, 64), (1, 8)))
    return dict(activation_cache=activation_cache, token_ids=token_ids, cotangent=cotangent, adapter_b=adapter_b, first_b=first_b, second_b=second_b, adapter_a=adapter_a, first_a=first_a, second_a=second_a, resident=resident, block_owner=block_owner, next_rows=next_rows)


adapter_scale = 4.0
rate = 0.2
beta_one = 0.9
beta_two = 0.999
bias_one = 1.0 - 0.9 ** 20
bias_two = 1.0 - 0.999 ** 20
eps_adam = 1e-08

def adam_step(param, first, second, grad):
    first_new = beta_one * first + (1.0 - beta_one) * grad
    second_new = beta_two * second + (1.0 - beta_two) * grad * grad
    update = first_new / bias_one / (jnp.sqrt(second_new / bias_two) + eps_adam)
    return (param - rate * update).astype(jnp.bfloat16)

def reference(activation_cache, token_ids, cotangent, adapter_b, first_b, second_b, adapter_a, first_a, second_a, resident, block_owner, next_rows):
    inverse_root = 1.0 / math.sqrt(D)
    highest_precision = lax.Precision.HIGHEST

    def one_worker(items):
        cache, chosen, incoming_gradient, factor_b, mom_b1, mom_b2, factor_a, mom_a1, mom_a2 = items
        selected_rows = jnp.take(cache, chosen, axis=0).astype(jnp.float32)
        incoming_gradient = incoming_gradient.astype(jnp.float32)
        hidden_state = jnp.dot(selected_rows, factor_b.T, precision=highest_precision) * inverse_root
        upstream_gradient = jnp.dot(incoming_gradient, factor_a.T, precision=highest_precision)
        gradient_left = adapter_scale / WORKER_TOKENS * jnp.dot(hidden_state.T, incoming_gradient, precision=highest_precision)
        gradient_right = adapter_scale * inverse_root / WORKER_TOKENS * jnp.dot(upstream_gradient.T, selected_rows, precision=highest_precision)
        return (adam_step(factor_b, mom_b1, mom_b2, gradient_right), adam_step(factor_a, mom_a1, mom_a2, gradient_left))
    new_b, new_a = lax.map(one_worker, (activation_cache, token_ids, cotangent, adapter_b, first_b, second_b, adapter_a, first_a, second_a))
    left = new_b.reshape(WORKER_COUNT * R, D)

    def one_block(items):
        position, owner = items
        right = lax.dynamic_slice_in_dim(new_a, (owner * FB).astype(jnp.int32), FB, 2).reshape(WORKER_COUNT * R, FB)
        weight_change = lax.dot_general(left, right, (((0,), (0,)), ((), ())), preferred_element_type=jnp.float32)
        stored_weight = lax.dynamic_slice_in_dim(resident, (position * FB).astype(jnp.int32), FB, 1)
        refreshed_block = (stored_weight.astype(jnp.float32) + adapter_scale / WORKER_COUNT * weight_change).astype(jnp.bfloat16)
        block_proj = (jnp.dot(next_rows, refreshed_block, preferred_element_type=jnp.float32) * inverse_root).astype(jnp.bfloat16)
        return (refreshed_block, block_proj)
    positions = jnp.arange(NB, dtype=jnp.int32)
    blocks_new, blocks_proj = lax.map(one_block, (positions, block_owner.astype(jnp.int32)))
    merged = jnp.transpose(blocks_new, (1, 0, 2)).reshape(D, NB * FB)
    projected = jnp.transpose(blocks_proj, (1, 0, 2)).reshape(NEXT, NB * FB)
    return (merged, projected)
```

```python
import math

import jax
import jax.numpy as jnp
from jax import lax
from jax.experimental import pallas as pl
from jax.experimental.pallas import tpu as pltpu
from jax.sharding import PartitionSpec as P

D = 8192
WORKER_TOKENS = 128
F32 = jnp.float32
BF16 = jnp.bfloat16
MESH = pl.DeviceIdType.MESH

adapter_scale = 4.0
rate = 0.2
beta_one = 0.9
beta_two = 0.999
bias_one = 1.0 - 0.9**20
bias_two = 1.0 - 0.999**20
eps_adam = 1e-08

NZ, NY, NX = 8, 2, 4
LANE = 128


def adam_step(param, first, second, grad):
    first_new = beta_one * first + (1.0 - beta_one) * grad
    second_new = beta_two * second + (1.0 - beta_two) * grad * grad
    update = first_new / bias_one / (jnp.sqrt(second_new / bias_two) + eps_adam)
    return param - rate * update


def split3(v):
    hi = v.astype(BF16)
    rest = v - hi.astype(F32)
    mid = rest.astype(BF16)
    low = (rest - mid.astype(F32)).astype(BF16)
    return jnp.concatenate([hi, mid, low], axis=0)


def sum3(v):
    n = v.shape[0] // 3
    return v[:n] + v[n : 2 * n] + v[2 * n :]


def dot(a, b):
    return lax.dot_general(a, b, (((1,), (0,)), ((), ())), preferred_element_type=F32)


def dot_nt(a, b):
    return lax.dot_general(a, b, (((1,), (1,)), ((), ())), preferred_element_type=F32)


class Gather:
    def __init__(self, ref, lanes, rs, ss, first, pos, n):
        self.ref, self.lanes, self.rs, self.ss, self.n = ref, lanes, rs, ss, n
        self.z, self.y, self.x = pos
        self.first = first
        self.na, self.nb = (NX, NZ) if first == "x" else (NZ, NX)
        self.a, self.b = (self.x, self.z) if first == "x" else (self.z, self.x)

    def index(self, y, a, b):
        z, x = (b, a) if self.first == "x" else (a, b)
        return (z * NY + y) * NX + x

    def view(self, v):
        if self.lanes is None:
            return self.ref.at[v]
        return self.ref.at[v, :, self.lanes]

    def copy(self, v, dest):
        return pltpu.make_async_remote_copy(
            self.view(v), self.view(v), self.ss, self.rs.at[v], device_id=(dest, self.n), device_id_type=MESH
        )

    def to_a(self, v, d):
        self.copy(v, self.index(self.y, (self.a + d + self.na) % self.na, self.b)).start()

    def to_b(self, v, d):
        self.copy(v, self.index(self.y, self.a, (self.b + d + self.nb) % self.nb)).start()

    def arrived(self, v):
        self.copy(v, self.index(1 - self.y, self.a, self.b)).wait_recv()

    def begin(self):
        me = self.index(self.y, self.a, self.b)
        self.copy(me, self.index(1 - self.y, self.a, self.b)).start()
        self.spread(me)

    def spread(self, v):
        self.to_a(v, 1)
        self.to_a(v, -1)
        self.to_b(v, 1)
        self.to_b(v, -1)

    def pair(self):
        v = self.index(1 - self.y, self.a, self.b)
        self.arrived(v)
        self.spread(v)

    def ring_a(self, s):
        for y in range(NY):
            for way in (1, -1):
                lim = self.na // 2 - (y == (1 if way == 1 else 0))
                if s <= lim:
                    v = self.index(y, (self.a - way * s + self.na) % self.na, self.b)
                    self.arrived(v)
                    if s < lim:
                        self.to_a(v, way)
                    self.to_b(v, 1)
                    self.to_b(v, -1)

    def ring_b(self, s):
        def step(q, _):
            for y in range(NY):
                for way in (1, -1):
                    lim = self.nb // 2 - (y == (1 if way == 1 else 0))
                    if s <= lim:
                        v = self.index(y, q, (self.b - way * s + self.nb) % self.nb)
                        self.arrived(v)
                        if s < lim:
                            self.to_b(v, way)
            return 0

        lax.fori_loop(0, self.na, step, 0)

    def sent(self):
        count = self.ref.shape[0] - 1
        if self.lanes is None:
            r = self.ref.at[pl.ds(0, count)]
        else:
            r = self.ref.at[pl.ds(0, count), :, self.lanes]
        pltpu.make_async_copy(r, r, self.ss).wait()


def kernel(
    tok_ref, owner_ref, cache_h, cot_h, ab_h, fb_h, sb_h, aa_h, fa_h, sa_h, res_h, nxt_h,
    merged_h, proj_h,
    cache, cot, ab, fb, sb, aa, fa, sa, res,
    pb, gb, gn, na, s1, bl, st, af, nbt, nrc, mg, px, pxr, po, rsrc, rrcv, pj,
    in_sem, pb_s, pb_r, gb0_r, gb1_r, gn_r, g_s, s1_s, s1_r, s2_s, s2_r, s3_s, s3_r, px_s, px_r, rr_s, rr_r, loc_s,
):
    w = lax.axis_index("wide")
    n = lax.axis_index("narrow")
    x = w % NX
    y = (w // NX) % NY
    z = w // (NX * NY)
    yh = n // 2
    c = n % 2
    nw = NZ * NY * NX
    inverse_root = 1.0 / math.sqrt(D)

    bar = pltpu.get_barrier_semaphore()

    def sig_w(d, _):
        pl.semaphore_signal(bar, inc=1, device_id=((w + d) % nw, n), device_id_type=MESH)
        return 0

    def sig_n(d, _):
        pl.semaphore_signal(bar, inc=1, device_id=(w, (n + d) % 8), device_id_type=MESH)
        return 0

    lax.fori_loop(1, nw, sig_w, 0)
    lax.fori_loop(1, 8, sig_n, 0)

    loads = {}
    pairs = (
        ("ab", ab_h.at[0], ab), ("cache", cache_h.at[0], cache), ("aa", aa_h.at[0], aa), ("cot", cot_h.at[0], cot),
        ("nxt", nxt_h, gn.at[w]), ("fb", fb_h.at[0], fb), ("sb", sb_h.at[0], sb), ("fa", fa_h.at[0], fa),
        ("sa", sa_h.at[0], sa), ("res", res_h, res),
    )
    for i, (name, src, dst) in enumerate(pairs):
        loads[name] = pltpu.make_async_copy(src, dst, in_sem.at[i])
        loads[name].start()

    oht = (lax.broadcasted_iota(jnp.int32, (128, 128), 0) == tok_ref[...]).astype(F32).astype(BF16)
    loads["ab"].wait()
    loads["cache"].wait()
    hp = sum3(dot_nt(split3(ab[...]), cache[...]))
    ht = sum3(dot(split3(hp), oht))
    loads["aa"].wait()
    loads["cot"].wait()
    ut = sum3(dot_nt(split3(aa[...]), cot[...]))
    qp = sum3(dot_nt(split3(ut), oht))
    pb[n] = jnp.concatenate([ht, qp], axis=0)

    pl.semaphore_wait(bar, nw - 1 + 7)

    def pb_copy(d):
        return pltpu.make_async_remote_copy(
            pb.at[n], pb.at[n], pb_s, pb_r, device_id=(w, (n + d) % 8), device_id_type=MESH
        )

    def pb_send(d, _):
        pb_copy(d).start()
        return 0

    lax.fori_loop(1, 8, pb_send, 0)

    pos = (z, y, x)
    gath_n = Gather(gn, None, gn_r, g_s.at[0], "z", pos, n)
    gath_0 = Gather(gb, pl.ds(0, 512), gb0_r, g_s.at[1], "z", pos, n)
    gath_1 = Gather(gb, pl.ds(512, 512), gb1_r, g_s.at[2], "x", pos, n)

    loads["nxt"].wait()
    gath_n.begin()
    gath_n.pair()

    r7 = pb.at[pl.ds(0, 7)]
    pltpu.make_async_copy(r7, r7, pb_r).wait()
    total = pb[0]
    for i in range(1, 8):
        total = total + pb[i]
    hid = total[:16] * inverse_root
    qsum = total[16:]

    grad_b = adapter_scale * inverse_root / WORKER_TOKENS * sum3(dot(split3(qsum), cache[...]))
    loads["fb"].wait()
    loads["sb"].wait()
    gb[w] = adam_step(ab[...], fb[...], sb[...], grad_b).astype(BF16)
    gath_0.begin()
    gath_1.begin()

    hs = split3(hid)
    loads["fa"].wait()
    loads["sa"].wait()
    cols = cot.shape[1]
    na[:, 4608:] = jnp.zeros((16, 128), F32)
    edges = (0, 1152, 2304, 3456, cols)
    for lo, hi in zip(edges[:-1], edges[1:]):
        grad_a = adapter_scale / WORKER_TOKENS * sum3(dot(hs, cot[:, lo:hi]))
        na[:, lo:hi] = adam_step(aa[:, lo:hi], fa[:, lo:hi], sa[:, lo:hi], grad_a)
    fbk = cols // 8
    for k in range(8):
        base = fbk * k // LANE * LANE
        shift = fbk * k - base
        win = na[:, base : base + 768]
        if shift:
            win = pltpu.roll(win, 768 - shift, 1)
        blk = win[:, :640].astype(BF16)
        for t in range(5):
            s1[t, k] = blk[:, t * LANE : (t + 1) * LANE]

    own8 = pl.ds(n * 8, 8)
    holders = ((0, 0), (1, 2), (2, 4), (3, 6), (4, 1), (4, 5))

    def s1_copy(i):
        t, dest = holders[i]
        return pltpu.make_async_remote_copy(
            s1.at[t], bl.at[own8], s1_s.at[i], s1_r, device_id=(w, dest), device_id_type=MESH
        )

    for i, (t, dest) in enumerate(holders):

        @pl.when(n != dest)
        def _():
            s1_copy(i).start()

        @pl.when(n == dest)
        def _():
            bl[own8] = s1[t]

    gath_0.pair()
    gath_1.pair()
    gath_n.ring_a(1)
    gath_0.ring_a(1)
    gath_1.ring_a(1)
    gath_n.ring_a(2)
    gath_0.ring_a(2)
    gath_1.ring_a(2)

    even = c == 0
    holds = jnp.logical_or(even, jnp.logical_or(n == 1, n == 5))
    y4 = n // 4
    gets = jnp.logical_or(even, jnp.logical_or(jnp.logical_and(n == 1, y == 0), jnp.logical_and(n == 5, y == 1)))
    tile = jnp.where(even, yh, 4)

    @pl.when(holds)
    def _():
        r = bl.at[pl.ds(0, 56)]
        pltpu.make_async_copy(r, r, s1_r).wait()

        def pick(j, _):
            st[j] = bl[owner_ref[j]]
            return 0

        lax.fori_loop(0, nw, pick, 0)

    lane = pl.ds(pl.multiple_of(tile * LANE, LANE), LANE)

    def s2_copy(j):
        return pltpu.make_async_remote_copy(
            st.at[j], af.at[w, :, lane], s2_s, s2_r, device_id=(j, n), device_id_type=MESH
        )

    @pl.when(even)
    def _():
        def send(d, _):
            s2_copy((w + d) % nw).start()
            return 0

        lax.fori_loop(1, nw, send, 0)

    @pl.when(jnp.logical_and(holds, jnp.logical_not(even)))
    def _():
        def send(d, _):
            j = (w + d) % nw

            @pl.when((j // NX) % NY == y4)
            def _():
                s2_copy(j).start()

            return 0

        lax.fori_loop(1, nw, send, 0)

    @pl.when(gets)
    def _():
        own = pltpu.make_async_copy(st.at[w], af.at[w, :, lane], loc_s)
        own.start()
        own.wait()

    gath_n.ring_a(3)
    gath_0.ring_a(3)
    gath_n.ring_a(4)
    gath_0.ring_a(4)
    gath_1.ring_b(1)
    gath_n.ring_b(1)
    gath_0.ring_b(1)
    gath_1.ring_b(2)

    @pl.when(gets)
    def _():
        r = af.at[pl.ds(0, nw - 1), :, lane]
        pltpu.make_async_copy(r, r, s2_r).wait()

    def piece(t, half):
        return af.at[pl.ds(half * (nw // 2), nw // 2), :, pl.ds(pl.multiple_of(t * LANE, LANE), LANE)]

    up, down, far = (yh + 1) % 4, (yh + 3) % 4, (yh + 2) % 4

    def s3(t, half, slot, sem, dest):
        return pltpu.make_async_remote_copy(
            piece(t, half), piece(t, half), s3_s.at[sem], s3_r.at[slot], device_id=(w, dest), device_id_type=MESH
        )

    partner = yh * 2 + 1 - c
    d4 = (yh - 2 * y + 4) % 4
    even_sends = (
        (yh, 0, 2, 0, up * 2), (yh, 1, 5, 1, down * 2), (yh, 1, 3, 2, up * 2), (yh, 0, 4, 3, down * 2),
        (yh, 0, 0, 4, partner), (yh, 1, 1, 5, partner),
    )
    src_sends = (
        (4, 0, 8, 0, up * 2 + 1), (4, 1, 9, 1, down * 2 + 1), (4, 1, 9, 2, up * 2 + 1), (4, 0, 8, 3, down * 2 + 1),
        (4, 0, 8, 4, partner), (4, 1, 9, 5, partner),
    )

    @pl.when(even)
    def _():
        for args in even_sends:
            s3(*args).start()

    @pl.when(jnp.logical_and(c == 1, d4 == 0))
    def _():
        for args in src_sends:
            s3(*args).start()

    gath_n.ring_b(2)
    gath_0.ring_b(2)

    @pl.when(even)
    def _():
        s3(down, 0, 2, 0, partner).wait_recv()
        s3(down, 0, 6, 6, up * 2).start()
        s3(down, 0, 2, 7, partner).start()
        s3(up, 1, 5, 0, partner).wait_recv()
        s3(up, 1, 7, 8, down * 2).start()
        s3(up, 1, 5, 9, partner).start()

    @pl.when(jnp.logical_and(c == 1, d4 == 1))
    def _():
        s3(4, 0, 8, 0, partner).wait_recv()
        s3(4, 0, 8, 0, up * 2 + 1).start()
        s3(4, 0, 8, 1, partner).start()
        s3(4, 1, 9, 0, partner).wait_recv()
        s3(4, 1, 9, 2, partner).start()

    @pl.when(jnp.logical_and(c == 1, d4 == 3))
    def _():
        s3(4, 1, 9, 0, partner).wait_recv()
        s3(4, 1, 9, 0, down * 2 + 1).start()
        s3(4, 1, 9, 1, partner).start()
        s3(4, 0, 8, 0, partner).wait_recv()
        s3(4, 0, 8, 2, partner).start()

    @pl.when(even)
    def _():
        s3(down, 1, 3, 0, partner).wait_recv()
        s3(down, 1, 3, 10, partner).start()
        s3(up, 0, 4, 0, partner).wait_recv()
        s3(up, 0, 4, 11, partner).start()

    gath_1.ring_b(3)
    gath_1.ring_b(4)

    for h in range(4):
        for k in range(2):
            i = 2 * h + k
            rows = gn[pl.ds(i * 8, 8)].astype(F32).reshape(64, gn.shape[2]).astype(BF16)
            nrc[k, h * 64 : (h + 1) * 64] = rows

    for t in range(8):
        part = gb[:, :, t * LANE : (t + 1) * LANE].reshape(nw * 16, LANE)
        nbt[t * LANE : (t + 1) * LANE, :] = part.T

    @pl.when(even)
    def _():
        s3(far, 0, 6, 0, partner).wait_recv()
        s3(far, 0, 6, 12, partner).start()
        s3(far, 1, 7, 0, partner).wait_recv()
        s3(far, 1, 7, 13, partner).start()
        s3(4, 0, 8, 0, partner).wait_recv()
        s3(4, 1, 9, 0, partner).wait_recv()

    @pl.when(jnp.logical_and(c == 1, d4 == 2))
    def _():
        s3(4, 0, 8, 0, partner).wait_recv()
        s3(4, 0, 8, 0, partner).start()
        s3(4, 1, 9, 0, partner).wait_recv()
        s3(4, 1, 9, 1, partner).start()

    @pl.when(c == 1)
    def _():
        for t, half, slot in (
            (yh, 0, 0), (yh, 1, 1), (down, 0, 2), (down, 1, 3), (up, 0, 4), (up, 1, 5), (far, 0, 6), (far, 1, 7),
        ):
            s3(t, half, slot, 0, partner).wait_recv()

    fbw = res.shape[1]
    loads["res"].wait()

    def merge(t, _):
        rows = pl.ds(pl.multiple_of(t * 128, 128), 128)
        delta = dot(nbt[rows, :], af[...].reshape(nw * 16, 640))
        mg[rows, :] = (res[rows, :].astype(F32) + adapter_scale / nw * delta[:, :fbw]).astype(BF16)
        return 0

    lax.fori_loop(0, res.shape[0] // 128, merge, 0)
    out_m = pltpu.make_async_copy(mg, merged_h, in_sem.at[0])
    out_m.start()

    px[...] = dot(nrc[1 - c], mg[...]).astype(BF16)
    xcopy = pltpu.make_async_remote_copy(px, pxr, px_s, px_r, device_id=(w, partner), device_id_type=MESH)
    xcopy.start()
    po[...] = dot(nrc[c], mg[...]).reshape(po.shape)
    xcopy.wait_recv()
    for h in range(4):
        both = po[h] + pxr[h * 64 : (h + 1) * 64].astype(F32)
        po[h] = both
        rsrc[h] = both.astype(BF16)

    def rr_copy(d):
        h = (yh + d) % 4
        return pltpu.make_async_remote_copy(
            rsrc.at[h], rrcv.at[yh], rr_s.at[d], rr_r, device_id=(w, h * 2 + c), device_id_type=MESH
        )

    for d in (2, 1, 3):
        rr_copy(d).start()
    r3 = rrcv.at[pl.ds(0, 3)]
    pltpu.make_async_copy(r3, r3, rr_r).wait()
    acc = po[yh]
    for d in (1, 2, 3):
        acc = acc + rrcv[(yh + d) % 4].astype(F32)
    pj[...] = (acc * inverse_root).astype(BF16)
    out_p = pltpu.make_async_copy(pj, proj_h, in_sem.at[1])
    out_p.start()

    pltpu.make_async_copy(r7, r7, pb_s).wait()
    gath_n.sent()
    gath_0.sent()
    gath_1.sent()
    for i, (t, dest) in enumerate(holders):

        @pl.when(n != dest)
        def _():
            s1_copy(i).wait_send()

    @pl.when(even)
    def _():
        r = st.at[pl.ds(0, nw - 1)]
        pltpu.make_async_copy(r, r, s2_s).wait()
        for i in range(14):
            s3(0, 0, 0, i, partner).wait_send()

    @pl.when(jnp.logical_and(holds, jnp.logical_not(even)))
    def _():
        @pl.when(gets)
        def _():
            r = st.at[pl.ds(0, nw // 2 - 1)]
            pltpu.make_async_copy(r, r, s2_s).wait()

        @pl.when(jnp.logical_not(gets))
        def _():
            r = st.at[pl.ds(0, nw // 2)]
            pltpu.make_async_copy(r, r, s2_s).wait()

    @pl.when(c == 1)
    def _():
        for i in range(2):
            s3(0, 0, 0, i, partner).wait_send()

        @pl.when(d4 != 2)
        def _():
            s3(0, 0, 0, 2, partner).wait_send()

        @pl.when(d4 == 0)
        def _():
            for i in range(3, 6):
                s3(0, 0, 0, i, partner).wait_send()

    xcopy.wait_send()
    for d in (2, 1, 3):
        rr_copy(d).wait_send()
    out_m.wait()
    out_p.wait()


def per_device(
    activation_cache, token_ids, cotangent, adapter_b, first_b, second_b, adapter_a, first_a, second_a, resident,
    block_owner, next_rows,
):
    dl = activation_cache.shape[2]
    cl = cotangent.shape[2]
    rl, fb = resident.shape
    nw = NZ * NY * NX
    anyspec = pl.BlockSpec(memory_space=pl.ANY)
    dma = pltpu.SemaphoreType.DMA
    vm = pltpu.VMEM
    scratch = [
        vm((128, dl), BF16), vm((128, cl), BF16), vm((16, dl), F32), vm((16, dl), F32), vm((16, dl), F32),
        vm((16, cl), F32), vm((16, cl), F32), vm((16, cl), F32), vm((rl, fb), BF16),
        vm((8, 32, 128), F32),
        vm((nw, 16, dl), BF16),
        vm((nw, 8, dl), BF16),
        vm((16, 4736), F32),
        vm((5, 8, 16, LANE), BF16),
        vm((nw, 16, LANE), BF16),
        vm((nw, 16, LANE), BF16),
        vm((nw, 16, 640), BF16),
        vm((dl, nw * 16), BF16),
        vm((2, 256, dl), BF16),
        vm((rl, fb), BF16),
        vm((256, fb), BF16), vm((256, fb), BF16),
        vm((4, 64, fb), F32),
        vm((4, 64, fb), BF16), vm((4, 64, fb), BF16),
        vm((64, fb), BF16),
        dma((10,)), dma(()), dma(()),
        dma((nw,)), dma((nw,)), dma((nw,)), dma((3,)),
        dma((6,)), dma(()), dma(()), dma(()),
        dma((14,)), dma((10,)),
        dma(()), dma(()), dma((4,)), dma(()), dma(()),
    ]
    return pl.pallas_call(
        kernel,
        out_shape=(jax.ShapeDtypeStruct((rl, fb), BF16), jax.ShapeDtypeStruct((64, fb), BF16)),
        in_specs=[pl.BlockSpec(memory_space=pltpu.VMEM), pl.BlockSpec(memory_space=pltpu.SMEM)] + [anyspec] * 10,
        out_specs=(anyspec, anyspec),
        scratch_shapes=scratch,
        compiler_params=pltpu.CompilerParams(collective_id=0, has_side_effects=True, vmem_limit_bytes=60 * 1024 * 1024),
        name="merge_step",
    )(
        token_ids, block_owner, activation_cache, cotangent, adapter_b, first_b, second_b, adapter_a, first_a, second_a,
        resident, next_rows,
    )


def solution(mesh):
    return jax.shard_map(
        per_device,
        mesh=mesh,
        in_specs=(
            P("wide", None, "narrow"),
            P("wide", None),
            P("wide", None, "narrow"),
            P("wide", None, "narrow"),
            P("wide", None, "narrow"),
            P("wide", None, "narrow"),
            P("wide", None, "narrow"),
            P("wide", None, "narrow"),
            P("wide", None, "narrow"),
            P("narrow", "wide"),
            P(),
            P("wide", "narrow"),
        ),
        out_specs=(P("narrow", "wide"), P("narrow", "wide")),
        check_vma=False,
    )
```

```python
import math

import jax
import jax.numpy as jnp
from jax import lax
from jax.experimental import pallas as pl
from jax.experimental.pallas import tpu as pltpu
from jax.sharding import PartitionSpec as P

D = 8192
WORKER_TOKENS = 128
F32 = jnp.float32
BF16 = jnp.bfloat16
MESH = pl.DeviceIdType.MESH

adapter_scale = 4.0
rate = 0.2
beta_one = 0.9
beta_two = 0.999
bias_one = 1.0 - 0.9**20
bias_two = 1.0 - 0.999**20
eps_adam = 1e-08

NZ, NY, NX = 8, 2, 4
LANE = 128


def adam_step(param, first, second, grad):
    first_new = beta_one * first + (1.0 - beta_one) * grad
    second_new = beta_two * second + (1.0 - beta_two) * grad * grad
    update = first_new / bias_one / (jnp.sqrt(second_new / bias_two) + eps_adam)
    return param - rate * update


def split3(v):
    hi = v.astype(BF16)
    rest = v - hi.astype(F32)
    mid = rest.astype(BF16)
    low = (rest - mid.astype(F32)).astype(BF16)
    return jnp.concatenate([hi, mid, low], axis=0)


def sum3(v):
    n = v.shape[0] // 3
    return v[:n] + v[n : 2 * n] + v[2 * n :]


def dot(a, b):
    return lax.dot_general(a, b, (((1,), (0,)), ((), ())), preferred_element_type=F32)


def dot_nt(a, b):
    return lax.dot_general(a, b, (((1,), (1,)), ((), ())), preferred_element_type=F32)


class Gather:
    def __init__(self, ref, lanes, rs, ss, first, pos, n):
        self.ref, self.lanes, self.rs, self.ss, self.n = ref, lanes, rs, ss, n
        self.z, self.y, self.x = pos
        self.first = first
        self.na, self.nb = (NX, NZ) if first == "x" else (NZ, NX)
        self.a, self.b = (self.x, self.z) if first == "x" else (self.z, self.x)

    def index(self, y, a, b):
        z, x = (b, a) if self.first == "x" else (a, b)
        return (z * NY + y) * NX + x

    def view(self, v):
        if self.lanes is None:
            return self.ref.at[v]
        return self.ref.at[v, :, self.lanes]

    def slot_b(self, s, way, y):
        return 3 + ((s - 1) * 2 + (way < 0)) * 2 + y

    def copy(self, v, dest, slot):
        return pltpu.make_async_remote_copy(
            self.view(v), self.view(v), self.ss, self.rs.at[slot], device_id=(dest, self.n), device_id_type=MESH
        )

    def to_b(self, v, way, s, y):
        dest = self.index(self.y, self.a, (self.b + way + self.nb) % self.nb)
        self.copy(v, dest, self.slot_b(s, way, y)).start()

    def arrived(self, slot, count):
        if self.lanes is None:
            r = self.ref.at[pl.ds(0, count)]
        else:
            r = self.ref.at[pl.ds(0, count), :, self.lanes]
        pltpu.make_async_copy(r, r, self.rs.at[slot]).wait()

    def begin(self):
        me = self.index(self.y, self.a, self.b)

        self.copy(me, self.index(1 - self.y, self.a, self.b), 0).start()
        self.along(me, self.y, 1)

    def along(self, v, y, slot):
        def send(d, _):
            self.copy(v, self.index(self.y, (self.a + d) % self.na, self.b), slot).start()
            return 0

        lax.fori_loop(1, self.na, send, 0)
        for way in (1, -1):
            self.to_b(v, way, 1, y)

    def pair(self):
        self.arrived(0, 1)
        self.along(self.index(1 - self.y, self.a, self.b), 1 - self.y, 2)

    def direct(self):
        for slot, y in ((1, self.y), (2, 1 - self.y)):
            self.arrived(slot, self.na - 1)

            def step(d, _):
                v = self.index(y, (self.a + d) % self.na, self.b)
                for way in (1, -1):
                    self.to_b(v, way, 1, y)
                return 0

            lax.fori_loop(1, self.na, step, 0)

    def ring_b(self, s):
        for y in range(NY):
            for way in (1, -1):
                lim = self.nb // 2 - (y == (1 if way == 1 else 0))
                if s <= lim:
                    self.arrived(self.slot_b(s, way, y), self.na)
                    if s < lim:

                        def step(q, _):
                            v = self.index(y, q, (self.b - way * s + self.nb) % self.nb)
                            self.to_b(v, way, s + 1, y)
                            return 0

                        lax.fori_loop(0, self.na, step, 0)

    def sent(self):
        count = self.ref.shape[0] - 1
        if self.lanes is None:
            r = self.ref.at[pl.ds(0, count)]
        else:
            r = self.ref.at[pl.ds(0, count), :, self.lanes]
        pltpu.make_async_copy(r, r, self.ss).wait()


def kernel(
    tok_h, owner_h, cache_h, cot_h, ab_h, fb_h, sb_h, aa_h, fa_h, sa_h, res_h, nxt_h,
    mg, pj,
    tok_ref, owner_ref, cache, cot, ab, fb, sb, aa, fa, sa, res,
    pb, gb, gn, na, s1, bl, st, rv, at, nr, px, pxr, po, rsrc, rrcv, rf, tx, tr, ts, tg, tt,
    in_sem, pb_s, pb_r, gb0_r, gb1_r, gn_r, g_s, t_s, t_r, tw_s, tw_r, rf_r, s1_s, s1_r, s2_s, s2_r, s3_s, s3_r, px_s, px_r, rr_s, rr_r, loc_s,
):
    w = lax.axis_index("wide")
    n = lax.axis_index("narrow")
    x = w % NX
    y = (w // NX) % NY
    z = w // (NX * NY)
    yh = n // 2
    c = n % 2
    nw = NZ * NY * NX
    inverse_root = 1.0 / math.sqrt(D)

    loads = {}
    pairs = (
        ("tok", tok_h, tok_ref), ("ab", ab_h.at[0], ab), ("cache", cache_h.at[0], cache), ("aa", aa_h.at[0], aa), ("cot", cot_h.at[0], cot),
        ("nxt", nxt_h, gn.at[w]), ("fb", fb_h.at[0], fb), ("sb", sb_h.at[0], sb), ("fa", fa_h.at[0], fa),
        ("sa", sa_h.at[0], sa), ("res", res_h, res),
        ("owner", owner_h, owner_ref),
    )
    for i, (name, src, dst) in enumerate(pairs):
        loads[name] = pltpu.make_async_copy(src, dst, in_sem.at[i])
        loads[name].start()

    bar = pltpu.get_barrier_semaphore()

    def sig_w(d, _):
        pl.semaphore_signal(bar, inc=1, device_id=((w + d) % nw, n), device_id_type=MESH)
        return 0

    def sig_n(d, _):
        pl.semaphore_signal(bar, inc=1, device_id=(w, (n + d) % 8), device_id_type=MESH)
        return 0

    lax.fori_loop(1, nw, sig_w, 0)
    lax.fori_loop(1, 8, sig_n, 0)

    loads["tok"].wait()
    oht = (lax.broadcasted_iota(jnp.int32, (128, 128), 0) == tok_ref[...]).astype(F32).astype(BF16)
    loads["ab"].wait()
    loads["cache"].wait()
    hp = sum3(dot_nt(split3(ab[...]), cache[...]))
    ht = sum3(dot(split3(hp), oht))
    loads["aa"].wait()
    loads["cot"].wait()
    ut = sum3(dot(split3(aa[...]), cot[...]))
    qp = sum3(dot_nt(split3(ut), oht))
    pb[n] = jnp.concatenate([ht, qp], axis=0).astype(BF16)

    pl.semaphore_wait(bar, nw - 1 + 7)

    def pb_copy(d):
        return pltpu.make_async_remote_copy(
            pb.at[n], pb.at[n], pb_s, pb_r, device_id=(w, (n + d) % 8), device_id_type=MESH
        )

    def pb_send(d, _):
        pb_copy(d).start()
        return 0

    lax.fori_loop(1, 8, pb_send, 0)

    pos = (z, y, x)
    gath_n = Gather(gn, None, gn_r, g_s.at[0], "z", pos, n)
    gath_0 = Gather(gb, pl.ds(0, 768), gb0_r, g_s.at[1], "z", pos, n)
    gath_1 = Gather(gb, pl.ds(768, 256), gb1_r, g_s.at[2], "x", pos, n)

    loads["nxt"].wait()
    gath_n.begin()
    gath_n.pair()

    r7 = pb.at[pl.ds(0, 7)]
    pltpu.make_async_copy(r7, r7, pb_r).wait()
    total = pb[0].astype(F32)
    for i in range(1, 8):
        total = total + pb[i].astype(F32)
    hid = total[:16] * inverse_root
    qsum = total[16:]

    grad_b = adapter_scale * inverse_root / WORKER_TOKENS * sum3(dot(split3(qsum), cache[...]))
    loads["fb"].wait()
    loads["sb"].wait()
    gb[w] = adam_step(ab[...], fb[...], sb[...], grad_b).astype(BF16)
    gath_0.begin()
    gath_1.begin()

    hs = split3(hid)
    loads["fa"].wait()
    loads["sa"].wait()
    cols = cot.shape[0]
    na[:, 4608:] = jnp.zeros((16, 128), F32)
    edges = (0, 1152, 2304, 3456, cols)
    for lo, hi in zip(edges[:-1], edges[1:]):
        grad_a = adapter_scale / WORKER_TOKENS * sum3(dot_nt(hs, cot[lo:hi, :]))
        na[:, lo:hi] = adam_step(aa[:, lo:hi], fa[:, lo:hi], sa[:, lo:hi], grad_a)
    fbk = cols // 8
    for k in range(8):
        base = fbk * k // LANE * LANE
        shift = fbk * k - base
        win = na[:, base : base + 768]
        if shift:
            win = pltpu.roll(win, 768 - shift, 1)
        blk = win[:, :640].astype(BF16)
        for t in range(5):
            s1[t, k] = blk[:, t * LANE : (t + 1) * LANE]

    own8 = pl.ds(n * 8, 8)
    holders = ((0, 0), (1, 2), (2, 4), (3, 6), (4, 1), (4, 5))

    def s1_copy(i):
        t, dest = holders[i]
        return pltpu.make_async_remote_copy(
            s1.at[t], bl.at[own8], s1_s.at[i], s1_r, device_id=(w, dest), device_id_type=MESH
        )

    for i, (t, dest) in enumerate(holders):

        @pl.when(n != dest)
        def _():
            s1_copy(i).start()

        @pl.when(n == dest)
        def _():
            bl[own8] = s1[t]

    gath_1.pair()
    gath_0.pair()
    gath_n.direct()
    gath_1.direct()
    gath_n.ring_b(1)

    even = c == 0
    holds = jnp.logical_or(even, jnp.logical_or(n == 1, n == 5))
    y4 = n // 4
    gets = jnp.logical_or(even, jnp.logical_or(jnp.logical_and(n == 1, y == 0), jnp.logical_and(n == 5, y == 1)))
    tile = jnp.where(even, yh, 4)

    @pl.when(holds)
    def _():
        r = bl.at[pl.ds(0, 56)]
        pltpu.make_async_copy(r, r, s1_r).wait()

        loads["owner"].wait()

        def pick(j, _):
            st[j] = bl[owner_ref[j]]
            return 0

        lax.fori_loop(0, nw, pick, 0)

    def s2_copy(j):
        return pltpu.make_async_remote_copy(
            st.at[j], rv.at[w], s2_s, s2_r, device_id=(j, n), device_id_type=MESH
        )

    @pl.when(even)
    def _():
        def send(d, _):
            s2_copy((w + d) % nw).start()
            return 0

        lax.fori_loop(1, nw, send, 0)

    @pl.when(jnp.logical_and(holds, jnp.logical_not(even)))
    def _():
        def send(d, _):
            j = (w + d) % nw

            @pl.when((j // NX) % NY == y4)
            def _():
                s2_copy(j).start()

            return 0

        lax.fori_loop(1, nw, send, 0)

    @pl.when(gets)
    def _():
        own = pltpu.make_async_copy(st.at[w], rv.at[w], loc_s)
        own.start()
        own.wait()

    gath_0.direct()
    gath_n.ring_b(2)
    for i in range(8):
        rows = gn[pl.ds(i * 8, 8)].astype(F32).reshape(64, gn.shape[2]).astype(BF16)
        nr[i // 2, i % 2] = rows

    loads["res"].wait()
    partner = yh * 2 + 1 - c
    px[...] = dot_nt(nr[:, 1 - c].reshape(256, nr.shape[3]), res[...]).astype(BF16)
    xcopy = pltpu.make_async_remote_copy(px, pxr, px_s, px_r, device_id=(w, partner), device_id_type=MESH)
    xcopy.start()

    for h in range(4):
        tx[h] = dot_nt(gb[w], nr[h].reshape(128, nr.shape[3])).astype(BF16)
    tr[n] = tx[yh]

    def t_copy(d):
        dest = (n + d) % 8
        return pltpu.make_async_remote_copy(
            tx.at[dest // 2], tr.at[n], t_s.at[d - 1], t_r, device_id=(w, dest), device_id_type=MESH
        )

    for d in range(1, 8):
        t_copy(d).start()

    po[...] = dot_nt(nr[:, c].reshape(256, nr.shape[3]), res[...]).reshape(po.shape)
    gath_1.ring_b(1)
    xcopy.wait_recv()
    for h in range(4):
        po[h] = po[h] + pxr[h * 64 : (h + 1) * 64].astype(F32)
    up, down, far = (yh + 1) % 4, (yh + 3) % 4, (yh + 2) % 4
    rsrc[2] = po[far].astype(BF16)

    def far_copy(i, h):
        half = pl.ds(32 * i, 32)
        return pltpu.make_async_remote_copy(
            rsrc.at[2, half], rf.at[i], rr_s.at[2 + i], rf_r.at[i], device_id=(w, h * 2 + c), device_id_type=MESH
        )

    def near_copy(i, h):
        return pltpu.make_async_remote_copy(
            rsrc.at[i], rrcv.at[i], rr_s.at[i], rr_r, device_id=(w, h * 2 + c), device_id_type=MESH
        )

    far_copy(0, up).start()
    far_copy(1, down).start()

    gath_0.ring_b(1)
    pltpu.make_async_copy(tr.at[pl.ds(0, 7)], tr.at[pl.ds(0, 7)], t_r).wait()
    tsum = tr[0].astype(F32)
    for i in range(1, 8):
        tsum = tsum + tr[i].astype(F32)
    ts[...] = tsum.astype(BF16)
    tg[w] = ts[...]

    def tw_send(d, _):
        pltpu.make_async_remote_copy(
            ts, tg.at[w], tw_s, tw_r, device_id=((w + d) % nw, n), device_id_type=MESH
        ).start()
        return 0

    lax.fori_loop(1, nw, tw_send, 0)

    far_copy(0, up).wait_recv()
    far_copy(1, down).wait_recv()
    toward = po[up]
    rsrc[0] = jnp.concatenate([toward[:32] + rf[0].astype(F32), toward[32:]], axis=0).astype(BF16)
    near_copy(0, up).start()
    toward = po[down]
    rsrc[1] = jnp.concatenate([toward[:32], toward[32:] + rf[1].astype(F32)], axis=0).astype(BF16)
    near_copy(1, down).start()

    @pl.when(gets)
    def _():
        r = rv.at[pl.ds(0, nw - 1)]
        pltpu.make_async_copy(r, r, s2_r).wait()
        right = rv[...].reshape(nw * 16, LANE).T

        @pl.when(even)
        def _():
            at[pl.ds(pl.multiple_of(yh * LANE, LANE), LANE), :] = right

        @pl.when(jnp.logical_not(even))
        def _():
            at[4 * LANE :, :] = right[: at.shape[0] - 4 * LANE]

    def piece(t, half):
        if isinstance(t, int) and t == 4:
            return at.at[pl.ds(t * LANE + half * 48, 48 - half * 16)]
        return at.at[pl.ds(pl.multiple_of(t * LANE + half * 64, 64), 64)]


    def s3(t, half, slot, sem, dest):
        return pltpu.make_async_remote_copy(
            piece(t, half), piece(t, half), s3_s.at[sem], s3_r.at[slot], device_id=(w, dest), device_id_type=MESH
        )

    d4 = (yh - 2 * y + 4) % 4
    even_sends = (
        (yh, 0, 2, 0, up * 2), (yh, 1, 5, 1, down * 2), (yh, 1, 3, 2, up * 2), (yh, 0, 4, 3, down * 2),
        (yh, 0, 0, 4, partner), (yh, 1, 1, 5, partner),
    )
    src_sends = (
        (4, 0, 8, 0, up * 2 + 1), (4, 1, 9, 1, down * 2 + 1), (4, 1, 9, 2, up * 2 + 1), (4, 0, 8, 3, down * 2 + 1),
        (4, 0, 8, 4, partner), (4, 1, 9, 5, partner),
    )

    @pl.when(even)
    def _():
        for args in even_sends:
            s3(*args).start()

    @pl.when(jnp.logical_and(c == 1, d4 == 0))
    def _():
        for args in src_sends:
            s3(*args).start()

    gath_1.ring_b(2)
    gath_0.ring_b(2)
    gath_1.ring_b(3)
    @pl.when(even)
    def _():
        s3(down, 0, 2, 0, partner).wait_recv()
        s3(down, 0, 6, 6, up * 2).start()
        s3(down, 0, 2, 7, partner).start()
        s3(up, 1, 5, 0, partner).wait_recv()
        s3(up, 1, 7, 8, down * 2).start()
        s3(up, 1, 5, 9, partner).start()

    @pl.when(jnp.logical_and(c == 1, d4 == 1))
    def _():
        s3(4, 0, 8, 0, partner).wait_recv()
        s3(4, 0, 8, 0, up * 2 + 1).start()
        s3(4, 0, 8, 1, partner).start()
        s3(4, 1, 9, 0, partner).wait_recv()
        s3(4, 1, 9, 2, partner).start()

    @pl.when(jnp.logical_and(c == 1, d4 == 3))
    def _():
        s3(4, 1, 9, 0, partner).wait_recv()
        s3(4, 1, 9, 0, down * 2 + 1).start()
        s3(4, 1, 9, 1, partner).start()
        s3(4, 0, 8, 0, partner).wait_recv()
        s3(4, 0, 8, 2, partner).start()

    gath_1.ring_b(4)
    @pl.when(even)
    def _():
        s3(down, 1, 3, 0, partner).wait_recv()
        s3(down, 1, 3, 10, partner).start()
        s3(up, 0, 4, 0, partner).wait_recv()
        s3(up, 0, 4, 11, partner).start()

    @pl.when(even)
    def _():
        s3(far, 0, 6, 0, partner).wait_recv()
        s3(far, 0, 6, 12, partner).start()
        s3(far, 1, 7, 0, partner).wait_recv()
        s3(far, 1, 7, 13, partner).start()
        s3(4, 0, 8, 0, partner).wait_recv()
        s3(4, 1, 9, 0, partner).wait_recv()

    @pl.when(jnp.logical_and(c == 1, d4 == 2))
    def _():
        s3(4, 0, 8, 0, partner).wait_recv()
        s3(4, 0, 8, 0, partner).start()
        s3(4, 1, 9, 0, partner).wait_recv()
        s3(4, 1, 9, 1, partner).start()

    @pl.when(c == 1)
    def _():
        for t, half, slot in (
            (yh, 0, 0), (yh, 1, 1), (down, 0, 2), (down, 1, 3), (up, 0, 4), (up, 1, 5), (far, 0, 6), (far, 1, 7),
        ):
            s3(t, half, slot, 0, partner).wait_recv()

    fbw = res.shape[0]
    for t in range(res.shape[1] // 256):
        part = slice(t * 256, (t + 1) * 256)
        delta = dot(at[...], gb[:, :, part].reshape(nw * 16, 256))
        mg[:, part] = (res[:, part].astype(F32) + adapter_scale / nw * delta[:fbw]).astype(BF16)

    rt = tg.at[pl.ds(0, nw - 1)]
    pltpu.make_async_copy(rt, rt, tw_r).wait()
    term = dot(at[...], tg[...].reshape(nw * 16, LANE))
    tt[...] = term.T.reshape(tt.shape)
    pltpu.make_async_copy(rrcv, rrcv, rr_r).wait()
    acc = po[yh] + rrcv[0].astype(F32) + rrcv[1].astype(F32)
    acc = acc + adapter_scale / nw * tt[c][:, :fbw]
    pj[...] = (acc * inverse_root).astype(BF16)

    @pl.when(jnp.logical_not(holds))
    def _():
        loads["owner"].wait()

    pltpu.make_async_copy(r7, r7, pb_s).wait()
    gath_n.sent()
    gath_0.sent()
    gath_1.sent()
    pltpu.make_async_copy(rt, rt, tw_s).wait()
    for d in range(1, 8):
        t_copy(d).wait_send()
    for i, (t, dest) in enumerate(holders):

        @pl.when(n != dest)
        def _():
            s1_copy(i).wait_send()

    @pl.when(even)
    def _():
        r = st.at[pl.ds(0, nw - 1)]
        pltpu.make_async_copy(r, r, s2_s).wait()
        for i in range(14):
            s3(0, 0, 0, i, partner).wait_send()

    @pl.when(jnp.logical_and(holds, jnp.logical_not(even)))
    def _():
        @pl.when(gets)
        def _():
            r = st.at[pl.ds(0, nw // 2 - 1)]
            pltpu.make_async_copy(r, r, s2_s).wait()

        @pl.when(jnp.logical_not(gets))
        def _():
            r = st.at[pl.ds(0, nw // 2)]
            pltpu.make_async_copy(r, r, s2_s).wait()

    for d, halves in ((0, (0, 1, 1, 0, 0, 1)), (1, (0, 0, 1)), (2, (0, 1)), (3, (1, 1, 0))):

        @pl.when(jnp.logical_and(c == 1, d4 == d))
        def _():
            for i, half in enumerate(halves):
                s3(4, half, 0, i, partner).wait_send()

    xcopy.wait_send()
    far_copy(0, up).wait_send()
    far_copy(1, down).wait_send()
    near_copy(0, up).wait_send()
    near_copy(1, down).wait_send()


def per_device(
    activation_cache, token_ids, cotangent, adapter_b, first_b, second_b, adapter_a, first_a, second_a, resident,
    block_owner, next_rows,
):
    dl = activation_cache.shape[2]
    cl = cotangent.shape[2]
    rl, fb = resident.shape
    nw = NZ * NY * NX
    anyspec = pl.BlockSpec(memory_space=pl.ANY)
    dma = pltpu.SemaphoreType.DMA
    vm = pltpu.VMEM
    scratch = [
        vm((1, 128), jnp.int32), pltpu.SMEM((nw,), jnp.int32),
        vm((128, dl), BF16), vm((cl, 128), BF16), vm((16, dl), F32), vm((16, dl), F32), vm((16, dl), F32),
        vm((16, cl), F32), vm((16, cl), F32), vm((16, cl), F32), vm((fb, rl), BF16),
        vm((8, 32, 128), BF16),
        vm((nw, 16, dl), BF16),
        vm((nw, 8, dl), BF16),
        vm((16, 4736), F32),
        vm((5, 8, 16, LANE), BF16),
        vm((nw, 16, LANE), BF16),
        vm((nw, 16, LANE), BF16),
        vm((nw, 16, LANE), BF16),
        vm((4 * LANE + 80, nw * 16), BF16),
        vm((4, 2, 64, dl), BF16),
        vm((256, fb), BF16), vm((256, fb), BF16),
        vm((4, 64, fb), F32),
        vm((3, 64, fb), BF16), vm((2, 64, fb), BF16),
        vm((2, 32, fb), BF16),
        vm((4, 16, LANE), BF16), vm((8, 16, LANE), BF16), vm((16, LANE), BF16), vm((nw, 16, LANE), BF16),
        vm((2, 64, 4 * LANE + 80), F32),
        dma((12,)), dma(()), dma(()),
        dma((11,)), dma((19,)), dma((11,)), dma((3,)),
        dma((7,)), dma(()), dma(()), dma(()), dma((2,)),
        dma((6,)), dma(()), dma(()), dma(()),
        dma((14,)), dma((10,)),
        dma(()), dma(()), dma((4,)), dma(()), dma(()),
    ]
    merged, projected = pl.pallas_call(
        kernel,
        out_shape=(pltpu.VMEM((fb, rl), BF16), pltpu.VMEM((64, fb), BF16)),
        in_specs=[anyspec] * 12,
        out_specs=(pl.BlockSpec(memory_space=pltpu.VMEM),) * 2,
        scratch_shapes=scratch,
        compiler_params=pltpu.CompilerParams(collective_id=0, has_side_effects=True, vmem_limit_bytes=60 * 1024 * 1024),
        name="merge_step",
    )(
        token_ids, block_owner, activation_cache, jnp.swapaxes(cotangent, 1, 2), adapter_b, first_b, second_b, adapter_a,
        first_a, second_a, resident.T, next_rows,
    )
    return merged.T, projected


def solution(mesh):
    return jax.shard_map(
        per_device,
        mesh=mesh,
        in_specs=(
            P("wide", None, "narrow"),
            P("wide", None),
            P("wide", None, "narrow"),
            P("wide", None, "narrow"),
            P("wide", None, "narrow"),
            P("wide", None, "narrow"),
            P("wide", None, "narrow"),
            P("wide", None, "narrow"),
            P("wide", None, "narrow"),
            P("narrow", "wide"),
            P(),
            P("wide", "narrow"),
        ),
        out_specs=(P("narrow", "wide"), P("narrow", "wide")),
        check_vma=False,
    )
```

```python
import math

import jax
import jax.numpy as jnp
from jax import lax
from jax.experimental import pallas as pl
from jax.experimental.pallas import tpu as pltpu
from jax.sharding import PartitionSpec as P

D = 8192
WORKER_TOKENS = 128
F32 = jnp.float32
BF16 = jnp.bfloat16
MESH = pl.DeviceIdType.MESH

adapter_scale = 4.0
rate = 0.2
beta_one = 0.9
beta_two = 0.999
bias_one = 1.0 - 0.9**20
bias_two = 1.0 - 0.999**20
eps_adam = 1e-08

NZ, NY, NX = 8, 2, 4
LANE = 128


def adam_step(param, first, second, grad):
    first_new = beta_one * first + (1.0 - beta_one) * grad
    second_new = beta_two * second + (1.0 - beta_two) * grad * grad
    update = first_new / bias_one / (jnp.sqrt(second_new / bias_two) + eps_adam)
    return param - rate * update


def split3(v):
    hi = v.astype(BF16)
    rest = v - hi.astype(F32)
    mid = rest.astype(BF16)
    low = (rest - mid.astype(F32)).astype(BF16)
    return jnp.concatenate([hi, mid, low], axis=0)


def sum3(v):
    n = v.shape[0] // 3
    return v[:n] + v[n : 2 * n] + v[2 * n :]


def dot(a, b):
    return lax.dot_general(a, b, (((1,), (0,)), ((), ())), preferred_element_type=F32)


def dot_nt(a, b):
    return lax.dot_general(a, b, (((1,), (1,)), ((), ())), preferred_element_type=F32)


class Gather:
    def __init__(self, ref, lanes, rs, ss, first, pos, n):
        self.ref, self.lanes, self.rs, self.ss, self.n = ref, lanes, rs, ss, n
        self.z, self.y, self.x = pos
        self.first = first
        self.na, self.nb = (NX, NZ) if first == "x" else (NZ, NX)
        self.a, self.b = (self.x, self.z) if first == "x" else (self.z, self.x)

    def index(self, y, a, b):
        z, x = (b, a) if self.first == "x" else (a, b)
        return (z * NY + y) * NX + x

    def view(self, v):
        if self.lanes is None:
            return self.ref.at[v]
        return self.ref.at[v, :, self.lanes]

    def slot_b(self, s, way, y):
        return 1 + self.na // 2 + ((s - 1) * 2 + (way < 0)) * 2 + y

    def copy(self, v, dest, slot):
        return pltpu.make_async_remote_copy(
            self.view(v), self.view(v), self.ss, self.rs.at[slot], device_id=(dest, self.n), device_id_type=MESH
        )

    def to_b(self, v, way, s, y):
        dest = self.index(self.y, self.a, (self.b + way + self.nb) % self.nb)
        self.copy(v, dest, self.slot_b(s, way, y)).start()

    def arrived(self, slot, count):
        if self.lanes is None:
            r = self.ref.at[pl.ds(0, count)]
        else:
            r = self.ref.at[pl.ds(0, count), :, self.lanes]
        pltpu.make_async_copy(r, r, self.rs.at[slot]).wait()

    def begin(self):
        me = self.index(self.y, self.a, self.b)

        self.copy(me, self.index(1 - self.y, self.a, self.b), 0).start()
        self.along(me, self.y)

    def steps(self, dist):
        return (dist,) if dist == self.na // 2 else (dist, -dist)

    def along(self, v, y):
        for way in (1, -1):
            self.to_b(v, way, 1, y)
        for dist in range(1, self.na // 2 + 1):
            for d in self.steps(dist):
                self.copy(v, self.index(self.y, (self.a + d + self.na) % self.na, self.b), dist).start()

    def pair(self):
        self.arrived(0, 1)
        self.along(self.index(1 - self.y, self.a, self.b), 1 - self.y)

    def direct(self, dist):
        self.arrived(dist, 2 * len(self.steps(dist)))
        for y in range(NY):
            for d in self.steps(dist):
                v = self.index(y, (self.a + d + self.na) % self.na, self.b)
                for way in (1, -1):
                    self.to_b(v, way, 1, y)

    def ring_b(self, s):
        for y in range(NY):
            for way in (1, -1):
                lim = self.nb // 2 - (y == (1 if way == 1 else 0))
                if s <= lim:
                    self.arrived(self.slot_b(s, way, y), self.na)
                    if s < lim:

                        def step(q, _):
                            v = self.index(y, q, (self.b - way * s + self.nb) % self.nb)
                            self.to_b(v, way, s + 1, y)
                            return 0

                        lax.fori_loop(0, self.na, step, 0)

    def sent(self):
        count = self.ref.shape[0] - 1
        if self.lanes is None:
            r = self.ref.at[pl.ds(0, count)]
        else:
            r = self.ref.at[pl.ds(0, count), :, self.lanes]
        pltpu.make_async_copy(r, r, self.ss).wait()


def kernel(
    tok_h, owner_h, cache_h, cot_h, ab_h, fb_h, sb_h, aa_h, fa_h, sa_h, res_h, nxt_h,
    mg, pj,
    tok_ref, owner_ref, cache, cot, ab, fb, sb, aa, fa, sa, res,
    pb, gb, gn, na, s1, bl, st, rv, at, nr, px, pxr, po, rsrc, rrcv, rf, tx, tr, ts, tg, tt,
    in_sem, pb_s, pb_r, gb0_r, gb1_r, gn_r, g_s, t_s, t_r, tw_s, tw_r, te_s, te_r, rf_r, s1_s, s1_r, s2_s, s2_r, s3_s, s3_r, px_s, px_r, rr_s, rr_r, loc_s,
):
    w = lax.axis_index("wide")
    n = lax.axis_index("narrow")
    x = w % NX
    y = (w // NX) % NY
    z = w // (NX * NY)
    yh = n // 2
    c = n % 2
    nw = NZ * NY * NX
    inverse_root = 1.0 / math.sqrt(D)

    loads = {}
    pairs = (
        ("tok", tok_h, tok_ref), ("ab", ab_h.at[0], ab), ("cache", cache_h.at[0], cache), ("aa", aa_h.at[0], aa), ("cot", cot_h.at[0], cot),
        ("nxt", nxt_h, gn.at[w]), ("fb", fb_h.at[0], fb), ("sb", sb_h.at[0], sb), ("fa", fa_h.at[0], fa),
        ("sa", sa_h.at[0], sa), ("res", res_h, res),
        ("owner", owner_h, owner_ref),
    )
    for i, (name, src, dst) in enumerate(pairs):
        loads[name] = pltpu.make_async_copy(src, dst, in_sem.at[i])
        loads[name].start()

    bar = pltpu.get_barrier_semaphore()

    def sig_w(d, _):
        pl.semaphore_signal(bar, inc=1, device_id=((w + d) % nw, n), device_id_type=MESH)
        return 0

    def sig_n(d, _):
        pl.semaphore_signal(bar, inc=1, device_id=(w, (n + d) % 8), device_id_type=MESH)
        return 0

    lax.fori_loop(1, nw, sig_w, 0)
    lax.fori_loop(1, 8, sig_n, 0)

    loads["tok"].wait()
    oht = (lax.broadcasted_iota(jnp.int32, (128, 128), 0) == tok_ref[...]).astype(F32).astype(BF16)
    loads["ab"].wait()
    loads["cache"].wait()
    hp = sum3(dot_nt(split3(ab[...]), cache[...]))
    ht = sum3(dot(split3(hp), oht))
    loads["aa"].wait()
    loads["cot"].wait()
    ut = sum3(dot(split3(aa[...]), cot[...]))
    qp = sum3(dot_nt(split3(ut), oht))
    pb[n] = jnp.concatenate([ht, qp], axis=0).astype(BF16)

    pl.semaphore_wait(bar, nw - 1 + 7)

    def pb_copy(d):
        return pltpu.make_async_remote_copy(
            pb.at[n], pb.at[n], pb_s, pb_r, device_id=(w, (n + d) % 8), device_id_type=MESH
        )

    def pb_send(d, _):
        pb_copy(d).start()
        return 0

    lax.fori_loop(1, 8, pb_send, 0)

    pos = (z, y, x)
    gath_n = Gather(gn, None, gn_r, g_s.at[2], "z", pos, n)
    gath_0 = Gather(gb, pl.ds(0, 768), gb0_r, g_s.at[0], "z", pos, n)
    gath_1 = Gather(gb, pl.ds(768, 256), gb1_r, g_s.at[1], "x", pos, n)

    loads["nxt"].wait()
    gath_n.begin()
    gath_n.pair()

    r7 = pb.at[pl.ds(0, 7)]
    pltpu.make_async_copy(r7, r7, pb_r).wait()
    total = pb[0].astype(F32)
    for i in range(1, 8):
        total = total + pb[i].astype(F32)
    hid = total[:16] * inverse_root
    qsum = total[16:]

    grad_b = adapter_scale * inverse_root / WORKER_TOKENS * sum3(dot(split3(qsum), cache[...]))
    loads["fb"].wait()
    loads["sb"].wait()
    gb[w] = adam_step(ab[...], fb[...], sb[...], grad_b).astype(BF16)

    hs = split3(hid)
    loads["fa"].wait()
    loads["sa"].wait()
    cols = cot.shape[0]
    na[:, 4608:] = jnp.zeros((16, 128), F32)
    edges = (0, 1152, 2304, 3456, cols)
    for lo, hi in zip(edges[:-1], edges[1:]):
        grad_a = adapter_scale / WORKER_TOKENS * sum3(dot_nt(hs, cot[lo:hi, :]))
        na[:, lo:hi] = adam_step(aa[:, lo:hi], fa[:, lo:hi], sa[:, lo:hi], grad_a)
    fbk = cols // 8
    for k in range(8):
        base = fbk * k // LANE * LANE
        shift = fbk * k - base
        win = na[:, base : base + 768]
        if shift:
            win = pltpu.roll(win, 768 - shift, 1)
        blk = win[:, :640].astype(BF16)
        for t in range(5):
            s1[t, k] = blk[:, t * LANE : (t + 1) * LANE]

    own8 = pl.ds(n * 8, 8)
    holders = ((0, 0), (1, 2), (2, 4), (3, 6), (4, 1), (4, 5))

    def s1_copy(i):
        t, dest = holders[i]
        return pltpu.make_async_remote_copy(
            s1.at[t], bl.at[own8], s1_s.at[i], s1_r, device_id=(w, dest), device_id_type=MESH
        )

    for i, (t, dest) in enumerate(holders):

        @pl.when(n != dest)
        def _():
            s1_copy(i).start()

        @pl.when(n == dest)
        def _():
            bl[own8] = s1[t]

    gath_n.direct(1)
    gath_n.direct(2)
    gath_n.direct(3)
    gath_n.direct(4)
    gath_0.begin()
    gath_1.begin()

    even = c == 0
    holds = jnp.logical_or(even, jnp.logical_or(n == 1, n == 5))
    y4 = n // 4
    gets = jnp.logical_or(even, jnp.logical_or(jnp.logical_and(n == 1, y == 0), jnp.logical_and(n == 5, y == 1)))
    tile = jnp.where(even, yh, 4)

    @pl.when(holds)
    def _():
        r = bl.at[pl.ds(0, 56)]
        pltpu.make_async_copy(r, r, s1_r).wait()

        loads["owner"].wait()

        def pick(j, _):
            st[j] = bl[owner_ref[j]]
            return 0

        lax.fori_loop(0, nw, pick, 0)

    def s2_copy(j):
        return pltpu.make_async_remote_copy(
            st.at[j], rv.at[w], s2_s, s2_r, device_id=(j, n), device_id_type=MESH
        )

    @pl.when(even)
    def _():
        def send(d, _):
            s2_copy((w + d) % nw).start()
            return 0

        lax.fori_loop(1, nw, send, 0)

    @pl.when(jnp.logical_and(holds, jnp.logical_not(even)))
    def _():
        def send(d, _):
            j = (w + d) % nw

            @pl.when((j // NX) % NY == y4)
            def _():
                s2_copy(j).start()

            return 0

        lax.fori_loop(1, nw, send, 0)

    @pl.when(gets)
    def _():
        own = pltpu.make_async_copy(st.at[w], rv.at[w], loc_s)
        own.start()
        own.wait()

    gath_n.ring_b(1)
    gath_1.pair()
    gath_0.pair()
    gath_n.ring_b(2)
    for i in range(8):
        rows = gn[pl.ds(i * 8, 8)].astype(F32).reshape(64, gn.shape[2]).astype(BF16)
        nr[i // 2, i % 2] = rows

    loads["res"].wait()
    partner = yh * 2 + 1 - c
    px[...] = dot_nt(nr[:, 1 - c].reshape(256, nr.shape[3]), res[...]).astype(BF16)
    xcopy = pltpu.make_async_remote_copy(px, pxr, px_s, px_r, device_id=(w, partner), device_id_type=MESH)
    xcopy.start()

    for h in range(4):
        tx[h] = dot_nt(gb[w], nr[h].reshape(128, nr.shape[3])).astype(BF16)
    leads = c == y

    @pl.when(leads)
    def _():
        tr[n] = tx[yh]

    def t_copy(d):
        h = (yh + d) % 4
        return pltpu.make_async_remote_copy(
            tx.at[h], tr.at[n], t_s.at[d], t_r, device_id=(w, h * 2 + y), device_id_type=MESH
        )

    for d in (2, 1, 3):
        t_copy(d).start()

    @pl.when(jnp.logical_not(leads))
    def _():
        t_copy(0).start()

    up, down, far = (yh + 1) % 4, (yh + 3) % 4, (yh + 2) % 4
    po[...] = dot_nt(nr[:, c].reshape(256, nr.shape[3]), res[...]).reshape(po.shape)
    xcopy.wait_recv()
    for h in range(4):
        po[h] = po[h] + pxr[h * 64 : (h + 1) * 64].astype(F32)
    rsrc[2] = po[far].astype(BF16)

    def far_copy(i, h):
        half = pl.ds(32 * i, 32)
        return pltpu.make_async_remote_copy(
            rsrc.at[2, half], rf.at[i], rr_s.at[2 + i], rf_r.at[i], device_id=(w, h * 2 + c), device_id_type=MESH
        )

    def near_copy(i, h):
        return pltpu.make_async_remote_copy(
            rsrc.at[i], rrcv.at[i], rr_s.at[i], rr_r, device_id=(w, h * 2 + c), device_id_type=MESH
        )

    far_copy(0, up).start()
    far_copy(1, down).start()
    gath_0.direct(1)
    gath_0.direct(2)
    gath_1.direct(1)
    gath_1.direct(2)
    @pl.when(gets)
    def _():
        r = rv.at[pl.ds(0, nw - 1)]
        pltpu.make_async_copy(r, r, s2_r).wait()
        right = rv[...].reshape(nw * 16, LANE).T

        @pl.when(even)
        def _():
            at[pl.ds(pl.multiple_of(yh * LANE, LANE), LANE), :] = right

        @pl.when(jnp.logical_not(even))
        def _():
            at[4 * LANE :, :] = right[: at.shape[0] - 4 * LANE]

    def piece(t, half):
        if isinstance(t, int) and t == 4:
            return at.at[pl.ds(t * LANE + half * 48, 48 - half * 16)]
        return at.at[pl.ds(pl.multiple_of(t * LANE + half * 64, 64), 64)]

    def s3(t, half, slot, sem, dest):
        return pltpu.make_async_remote_copy(
            piece(t, half), piece(t, half), s3_s.at[sem], s3_r.at[slot], device_id=(w, dest), device_id_type=MESH
        )

    d4 = (yh - 2 * y + 4) % 4
    even_sends = (
        (yh, 0, 2, 0, up * 2), (yh, 1, 5, 1, down * 2), (yh, 1, 3, 2, up * 2), (yh, 0, 4, 3, down * 2),
        (yh, 0, 0, 4, partner), (yh, 1, 1, 5, partner),
    )
    src_sends = (
        (4, 0, 8, 0, up * 2 + 1), (4, 1, 9, 1, down * 2 + 1), (4, 1, 9, 2, up * 2 + 1), (4, 0, 8, 3, down * 2 + 1),
        (4, 0, 8, 4, partner), (4, 1, 9, 5, partner),
    )

    @pl.when(even)
    def _():
        for args in even_sends:
            s3(*args).start()

    @pl.when(jnp.logical_and(c == 1, d4 == 0))
    def _():
        for args in src_sends:
            s3(*args).start()

    gath_0.direct(3)
    gath_0.direct(4)
    gath_1.ring_b(1)

    @pl.when(leads)
    def _():
        pltpu.make_async_copy(tr.at[pl.ds(0, 7)], tr.at[pl.ds(0, 7)], t_r).wait()
        tsum = tr[0].astype(F32)
        for i in range(1, 8):
            tsum = tsum + tr[i].astype(F32)
        ts[...] = tsum.astype(BF16)
        tg[w] = ts[...]

        def tw_send(d, _):
            pltpu.make_async_remote_copy(
                ts, tg.at[w], tw_s, tw_r, device_id=((w + d) % nw, n), device_id_type=MESH
            ).start()
            return 0

        lax.fori_loop(1, nw, tw_send, 0)

    @pl.when(even)
    def _():
        s3(down, 0, 2, 0, partner).wait_recv()
        s3(down, 0, 6, 6, up * 2).start()
        s3(down, 0, 2, 7, partner).start()
        s3(up, 1, 5, 0, partner).wait_recv()
        s3(up, 1, 7, 8, down * 2).start()
        s3(up, 1, 5, 9, partner).start()

    @pl.when(jnp.logical_and(c == 1, d4 == 1))
    def _():
        s3(4, 0, 8, 0, partner).wait_recv()
        s3(4, 0, 8, 0, up * 2 + 1).start()
        s3(4, 0, 8, 1, partner).start()
        s3(4, 1, 9, 0, partner).wait_recv()
        s3(4, 1, 9, 2, partner).start()

    @pl.when(jnp.logical_and(c == 1, d4 == 3))
    def _():
        s3(4, 1, 9, 0, partner).wait_recv()
        s3(4, 1, 9, 0, down * 2 + 1).start()
        s3(4, 1, 9, 1, partner).start()
        s3(4, 0, 8, 0, partner).wait_recv()
        s3(4, 0, 8, 2, partner).start()

    gath_0.ring_b(1)
    gath_1.ring_b(2)
    far_copy(0, up).wait_recv()
    far_copy(1, down).wait_recv()
    toward = po[up]
    rsrc[0] = jnp.concatenate([toward[:32] + rf[0].astype(F32), toward[32:]], axis=0).astype(BF16)
    near_copy(0, up).start()
    toward = po[down]
    rsrc[1] = jnp.concatenate([toward[:32], toward[32:] + rf[1].astype(F32)], axis=0).astype(BF16)
    near_copy(1, down).start()

    gath_1.ring_b(3)
    @pl.when(even)
    def _():
        s3(down, 1, 3, 0, partner).wait_recv()
        s3(down, 1, 3, 10, partner).start()
        s3(up, 0, 4, 0, partner).wait_recv()
        s3(up, 0, 4, 11, partner).start()

    @pl.when(even)
    def _():
        s3(far, 0, 6, 0, partner).wait_recv()
        s3(far, 0, 6, 12, partner).start()
        s3(far, 1, 7, 0, partner).wait_recv()
        s3(far, 1, 7, 13, partner).start()
        s3(4, 0, 8, 0, partner).wait_recv()
        s3(4, 1, 9, 0, partner).wait_recv()

    @pl.when(jnp.logical_and(c == 1, d4 == 2))
    def _():
        s3(4, 0, 8, 0, partner).wait_recv()
        s3(4, 0, 8, 0, partner).start()
        s3(4, 1, 9, 0, partner).wait_recv()
        s3(4, 1, 9, 1, partner).start()

    def te_copy(i):
        span = pl.ds((i * NY + c) * NX, NX)
        return pltpu.make_async_remote_copy(
            tg.at[span], tg.at[span], te_s, te_r, device_id=(w, partner), device_id_type=MESH
        )

    half_tg = tg.at[pl.ds(0, nw // 2)]

    @pl.when(leads)
    def _():
        r = tg.at[pl.ds(0, nw // 2 - 1)]
        pltpu.make_async_copy(r, r, tw_r).wait()

    @pl.when(jnp.logical_not(leads))
    def _():
        pltpu.make_async_copy(half_tg, half_tg, tw_r).wait()

    for i in range(NZ):
        te_copy(i).start()

    gath_1.ring_b(4)
    gath_0.ring_b(2)
    @pl.when(c == 1)
    def _():
        for t, half, slot in (
            (yh, 0, 0), (yh, 1, 1), (down, 0, 2), (down, 1, 3), (up, 0, 4), (up, 1, 5), (far, 0, 6), (far, 1, 7),
        ):
            s3(t, half, slot, 0, partner).wait_recv()

    fbw = res.shape[0]
    for t in range(res.shape[1] // 256):
        part = slice(t * 256, (t + 1) * 256)
        delta = dot(at[...], gb[:, :, part].reshape(nw * 16, 256))
        mg[:, part] = (res[:, part].astype(F32) + adapter_scale / nw * delta[:fbw]).astype(BF16)

    pltpu.make_async_copy(half_tg, half_tg, te_r).wait()
    term = dot(at[...], tg[...].reshape(nw * 16, LANE))
    tt[...] = term.T.reshape(tt.shape)
    pltpu.make_async_copy(rrcv, rrcv, rr_r).wait()
    acc = po[yh] + rrcv[0].astype(F32) + rrcv[1].astype(F32)
    acc = acc + adapter_scale / nw * tt[c][:, :fbw]
    pj[...] = (acc * inverse_root).astype(BF16)

    @pl.when(jnp.logical_not(holds))
    def _():
        loads["owner"].wait()

    pltpu.make_async_copy(r7, r7, pb_s).wait()
    gath_n.sent()
    gath_0.sent()
    gath_1.sent()
    pltpu.make_async_copy(half_tg, half_tg, te_s).wait()

    @pl.when(leads)
    def _():
        r = tg.at[pl.ds(0, nw - 1)]
        pltpu.make_async_copy(r, r, tw_s).wait()

    @pl.when(jnp.logical_not(leads))
    def _():
        t_copy(0).wait_send()

    for d in (1, 2, 3):
        t_copy(d).wait_send()
    for i, (t, dest) in enumerate(holders):

        @pl.when(n != dest)
        def _():
            s1_copy(i).wait_send()

    @pl.when(even)
    def _():
        r = st.at[pl.ds(0, nw - 1)]
        pltpu.make_async_copy(r, r, s2_s).wait()
        for i in range(14):
            s3(0, 0, 0, i, partner).wait_send()

    @pl.when(jnp.logical_and(holds, jnp.logical_not(even)))
    def _():
        @pl.when(gets)
        def _():
            r = st.at[pl.ds(0, nw // 2 - 1)]
            pltpu.make_async_copy(r, r, s2_s).wait()

        @pl.when(jnp.logical_not(gets))
        def _():
            r = st.at[pl.ds(0, nw // 2)]
            pltpu.make_async_copy(r, r, s2_s).wait()

    for d, halves in ((0, (0, 1, 1, 0, 0, 1)), (1, (0, 0, 1)), (2, (0, 1)), (3, (1, 1, 0))):

        @pl.when(jnp.logical_and(c == 1, d4 == d))
        def _():
            for i, half in enumerate(halves):
                s3(4, half, 0, i, partner).wait_send()

    xcopy.wait_send()
    far_copy(0, up).wait_send()
    far_copy(1, down).wait_send()
    near_copy(0, up).wait_send()
    near_copy(1, down).wait_send()


def per_device(
    activation_cache, token_ids, cotangent, adapter_b, first_b, second_b, adapter_a, first_a, second_a, resident,
    block_owner, next_rows,
):
    dl = activation_cache.shape[2]
    cl = cotangent.shape[2]
    rl, fb = resident.shape
    nw = NZ * NY * NX
    anyspec = pl.BlockSpec(memory_space=pl.ANY)
    dma = pltpu.SemaphoreType.DMA
    vm = pltpu.VMEM
    scratch = [
        vm((1, 128), jnp.int32), pltpu.SMEM((nw,), jnp.int32),
        vm((128, dl), BF16), vm((cl, 128), BF16), vm((16, dl), F32), vm((16, dl), F32), vm((16, dl), F32),
        vm((16, cl), F32), vm((16, cl), F32), vm((16, cl), F32), vm((fb, rl), BF16),
        vm((8, 32, 128), BF16),
        vm((nw, 16, dl), BF16),
        vm((nw, 8, dl), BF16),
        vm((16, 4736), F32),
        vm((5, 8, 16, LANE), BF16),
        vm((nw, 16, LANE), BF16),
        vm((nw, 16, LANE), BF16),
        vm((nw, 16, LANE), BF16),
        vm((4 * LANE + 80, nw * 16), BF16),
        vm((4, 2, 64, dl), BF16),
        vm((256, fb), BF16), vm((256, fb), BF16),
        vm((4, 64, fb), F32),
        vm((3, 64, fb), BF16), vm((2, 64, fb), BF16),
        vm((2, 32, fb), BF16),
        vm((4, 16, LANE), BF16), vm((8, 16, LANE), BF16), vm((16, LANE), BF16), vm((nw, 16, LANE), BF16),
        vm((2, 64, 4 * LANE + 80), F32),
        dma((12,)), dma(()), dma(()),
        dma((13,)), dma((19,)), dma((13,)), dma((3,)),
        dma((4,)), dma(()), dma(()), dma(()), dma(()), dma(()), dma((2,)),
        dma((6,)), dma(()), dma(()), dma(()),
        dma((14,)), dma((10,)),
        dma(()), dma(()), dma((4,)), dma(()), dma(()),
    ]
    merged, projected = pl.pallas_call(
        kernel,
        out_shape=(pltpu.VMEM((fb, rl), BF16), pltpu.VMEM((64, fb), BF16)),
        in_specs=[anyspec] * 12,
        out_specs=(pl.BlockSpec(memory_space=pltpu.VMEM),) * 2,
        scratch_shapes=scratch,
        compiler_params=pltpu.CompilerParams(collective_id=0, has_side_effects=True, vmem_limit_bytes=60 * 1024 * 1024),
        name="merge_step",
    )(
        token_ids, block_owner, activation_cache, jnp.swapaxes(cotangent, 1, 2), adapter_b, first_b, second_b, adapter_a,
        first_a, second_a, resident.T, next_rows,
    )
    return merged.T, projected


def solution(mesh):
    return jax.shard_map(
        per_device,
        mesh=mesh,
        in_specs=(
            P("wide", None, "narrow"),
            P("wide", None),
            P("wide", None, "narrow"),
            P("wide", None, "narrow"),
            P("wide", None, "narrow"),
            P("wide", None, "narrow"),
            P("wide", None, "narrow"),
            P("wide", None, "narrow"),
            P("wide", None, "narrow"),
            P("narrow", "wide"),
            P(),
            P("wide", "narrow"),
        ),
        out_specs=(P("narrow", "wide"), P("narrow", "wide")),
        check_vma=False,
    )
```

```python
import math

import jax
import jax.numpy as jnp
from jax import lax
from jax.experimental import pallas as pl
from jax.experimental.pallas import tpu as pltpu
from jax.sharding import PartitionSpec as P

D = 8192
WORKER_TOKENS = 128
F32 = jnp.float32
BF16 = jnp.bfloat16
MESH = pl.DeviceIdType.MESH

adapter_scale = 4.0
rate = 0.2
beta_one = 0.9
beta_two = 0.999
bias_one = 1.0 - 0.9**20
bias_two = 1.0 - 0.999**20
eps_adam = 1e-08

NZ, NY, NX = 8, 2, 4
LANE = 128


def adam_step(param, first, second, grad):
    first_new = beta_one * first + (1.0 - beta_one) * grad
    second_new = beta_two * second + (1.0 - beta_two) * grad * grad
    update = first_new / bias_one / (jnp.sqrt(second_new / bias_two) + eps_adam)
    return param - rate * update


def split3(v):
    hi = v.astype(BF16)
    rest = v - hi.astype(F32)
    mid = rest.astype(BF16)
    low = (rest - mid.astype(F32)).astype(BF16)
    return jnp.concatenate([hi, mid, low], axis=0)


def sum3(v):
    n = v.shape[0] // 3
    return v[:n] + v[n : 2 * n] + v[2 * n :]


def dot(a, b):
    return lax.dot_general(a, b, (((1,), (0,)), ((), ())), preferred_element_type=F32)


def dot_nt(a, b):
    return lax.dot_general(a, b, (((1,), (1,)), ((), ())), preferred_element_type=F32)


class Gather:
    def __init__(self, ref, lanes, rs, ss, first, pos, n):
        self.ref, self.lanes, self.rs, self.ss, self.n = ref, lanes, rs, ss, n
        self.z, self.y, self.x = pos
        self.first = first
        self.na, self.nb = (NX, NZ) if first == "x" else (NZ, NX)
        self.a, self.b = (self.x, self.z) if first == "x" else (self.z, self.x)

    def index(self, y, a, b):
        z, x = (b, a) if self.first == "x" else (a, b)
        return (z * NY + y) * NX + x

    def view(self, v):
        if self.lanes is None:
            return self.ref.at[v]
        return self.ref.at[v, :, self.lanes]

    def slot_b(self, s, way, y):
        return 1 + self.na // 2 + ((s - 1) * 2 + (way < 0)) * 2 + y

    def copy(self, v, dest, slot):
        return pltpu.make_async_remote_copy(
            self.view(v), self.view(v), self.ss, self.rs.at[slot], device_id=(dest, self.n), device_id_type=MESH
        )

    def to_b(self, v, way, s, y):
        dest = self.index(self.y, self.a, (self.b + way + self.nb) % self.nb)
        self.copy(v, dest, self.slot_b(s, way, y)).start()

    def arrived(self, slot, count):
        if self.lanes is None:
            r = self.ref.at[pl.ds(0, count)]
        else:
            r = self.ref.at[pl.ds(0, count), :, self.lanes]
        pltpu.make_async_copy(r, r, self.rs.at[slot]).wait()

    def begin(self):
        me = self.index(self.y, self.a, self.b)

        self.copy(me, self.index(1 - self.y, self.a, self.b), 0).start()
        self.along(me, self.y)

    def steps(self, dist):
        return (dist,) if dist == self.na // 2 else (dist, -dist)

    def along(self, v, y):
        for way in (1, -1):
            self.to_b(v, way, 1, y)
        for dist in range(1, self.na // 2 + 1):
            for d in self.steps(dist):
                self.copy(v, self.index(self.y, (self.a + d + self.na) % self.na, self.b), dist).start()

    def pair(self):
        self.arrived(0, 1)
        self.along(self.index(1 - self.y, self.a, self.b), 1 - self.y)

    def direct(self, dist):
        self.arrived(dist, 2 * len(self.steps(dist)))
        for y in range(NY):
            for d in self.steps(dist):
                v = self.index(y, (self.a + d + self.na) % self.na, self.b)
                for way in (1, -1):
                    self.to_b(v, way, 1, y)

    def ring_b(self, s):
        for y in range(NY):
            for way in (1, -1):
                lim = self.nb // 2 - (y == (1 if way == 1 else 0))
                if s <= lim:
                    self.arrived(self.slot_b(s, way, y), self.na)
                    if s < lim:

                        def step(q, _):
                            v = self.index(y, q, (self.b - way * s + self.nb) % self.nb)
                            self.to_b(v, way, s + 1, y)
                            return 0

                        lax.fori_loop(0, self.na, step, 0)

    def sent(self):
        count = self.ref.shape[0] - 1
        if self.lanes is None:
            r = self.ref.at[pl.ds(0, count)]
        else:
            r = self.ref.at[pl.ds(0, count), :, self.lanes]
        pltpu.make_async_copy(r, r, self.ss).wait()


def kernel(
    tok_h, owner_h, cache_h, cot_h, ab_h, fb_h, sb_h, aa_h, fa_h, sa_h, res_h, nxt_h,
    mg, pj,
    tok_ref, owner_ref, cache, cot, ab, fb, sb, aa, fa, sa, res,
    pb, gb, gn, na, s1, bl, st, rv, at, nr, px, pxr, po, rsrc, rrcv, rf, tx, tr, ts, tg, tt,
    in_sem, pb_s, pb_r, gb0_r, gb1_r, gn_r, g_s, t_s, t_r, tw_s, tw_r, te_s, te_r, rf_r, s1_s, s1_r, s2_s, s2_r, s3_s, s3_r, px_s, px_r, rr_s, rr_r, loc_s,
):
    w = lax.axis_index("wide")
    n = lax.axis_index("narrow")
    x = w % NX
    y = (w // NX) % NY
    z = w // (NX * NY)
    yh = n // 2
    c = n % 2
    nw = NZ * NY * NX
    inverse_root = 1.0 / math.sqrt(D)

    loads = {}
    pairs = (
        ("tok", tok_h, tok_ref), ("ab", ab_h.at[0], ab), ("cache", cache_h.at[0], cache), ("aa", aa_h.at[0], aa), ("cot", cot_h.at[0], cot),
        ("nxt", nxt_h, gn.at[w]), ("fb", fb_h.at[0], fb), ("sb", sb_h.at[0], sb), ("fa", fa_h.at[0], fa),
        ("sa", sa_h.at[0], sa), ("res", res_h, res),
        ("owner", owner_h, owner_ref),
    )
    for i, (name, src, dst) in enumerate(pairs):
        loads[name] = pltpu.make_async_copy(src, dst, in_sem.at[i])
        loads[name].start()

    bar = pltpu.get_barrier_semaphore()

    def sig_w(d, _):
        pl.semaphore_signal(bar, inc=1, device_id=((w + d) % nw, n), device_id_type=MESH)
        return 0

    def sig_n(d, _):
        pl.semaphore_signal(bar, inc=1, device_id=(w, (n + d) % 8), device_id_type=MESH)
        return 0

    lax.fori_loop(1, nw, sig_w, 0)
    lax.fori_loop(1, 8, sig_n, 0)

    loads["tok"].wait()
    oht = (lax.broadcasted_iota(jnp.int32, (128, 128), 0) == tok_ref[...]).astype(F32).astype(BF16)
    loads["ab"].wait()
    loads["cache"].wait()
    hp = sum3(dot_nt(split3(ab[...]), cache[...]))
    ht = sum3(dot(split3(hp), oht))
    loads["aa"].wait()
    loads["cot"].wait()
    ut = sum3(dot(split3(aa[...]), cot[...]))
    qp = sum3(dot_nt(split3(ut), oht))
    pb[n] = jnp.concatenate([ht, qp], axis=0).astype(BF16)

    pl.semaphore_wait(bar, nw - 1 + 7)

    def pb_copy(d):
        return pltpu.make_async_remote_copy(
            pb.at[n], pb.at[n], pb_s, pb_r, device_id=(w, (n + d) % 8), device_id_type=MESH
        )

    def pb_send(d, _):
        pb_copy(d).start()
        return 0

    lax.fori_loop(1, 8, pb_send, 0)

    pos = (z, y, x)
    gath_n = Gather(gn, None, gn_r, g_s.at[2], "z", pos, n)
    gath_0 = Gather(gb, pl.ds(0, 768), gb0_r, g_s.at[0], "z", pos, n)
    gath_1 = Gather(gb, pl.ds(768, 256), gb1_r, g_s.at[1], "x", pos, n)

    loads["nxt"].wait()
    gath_n.begin()
    gath_n.pair()

    r7 = pb.at[pl.ds(0, 7)]
    pltpu.make_async_copy(r7, r7, pb_r).wait()
    total = pb[0].astype(F32)
    for i in range(1, 8):
        total = total + pb[i].astype(F32)
    hid = total[:16] * inverse_root
    qsum = total[16:]

    grad_b = adapter_scale * inverse_root / WORKER_TOKENS * sum3(dot(split3(qsum), cache[...]))
    loads["fb"].wait()
    loads["sb"].wait()
    gb[w] = adam_step(ab[...], fb[...], sb[...], grad_b).astype(BF16)

    hs = split3(hid)
    loads["fa"].wait()
    loads["sa"].wait()
    cols = cot.shape[0]
    na[:, 4608:] = jnp.zeros((16, 128), F32)
    edges = (0, 1152, 2304, 3456, cols)
    for lo, hi in zip(edges[:-1], edges[1:]):
        grad_a = adapter_scale / WORKER_TOKENS * sum3(dot_nt(hs, cot[lo:hi, :]))
        na[:, lo:hi] = adam_step(aa[:, lo:hi], fa[:, lo:hi], sa[:, lo:hi], grad_a)
    fbk = cols // 8
    for k in range(8):
        base = fbk * k // LANE * LANE
        shift = fbk * k - base
        win = na[:, base : base + 768]
        if shift:
            win = pltpu.roll(win, 768 - shift, 1)
        blk = win[:, :640].astype(BF16)
        for t in range(5):
            s1[t, k] = blk[:, t * LANE : (t + 1) * LANE]

    own8 = pl.ds(n * 8, 8)
    holders = ((0, 0), (1, 2), (2, 4), (3, 6), (4, 1), (4, 5))

    def s1_copy(i):
        t, dest = holders[i]
        return pltpu.make_async_remote_copy(
            s1.at[t], bl.at[own8], s1_s.at[i], s1_r, device_id=(w, dest), device_id_type=MESH
        )

    for i, (t, dest) in enumerate(holders):

        @pl.when(n != dest)
        def _():
            s1_copy(i).start()

        @pl.when(n == dest)
        def _():
            bl[own8] = s1[t]

    gath_n.direct(1)
    gath_n.direct(2)
    gath_n.direct(3)
    gath_n.direct(4)
    gath_0.begin()
    gath_1.begin()

    even = c == 0
    holds = jnp.logical_or(even, jnp.logical_or(n == 1, n == 5))
    y4 = n // 4
    gets = jnp.logical_or(even, jnp.logical_or(jnp.logical_and(n == 1, y == 0), jnp.logical_and(n == 5, y == 1)))
    tile = jnp.where(even, yh, 4)

    @pl.when(holds)
    def _():
        r = bl.at[pl.ds(0, 56)]
        pltpu.make_async_copy(r, r, s1_r).wait()

        loads["owner"].wait()

        def pick(j, _):
            st[j] = bl[owner_ref[j]]
            return 0

        lax.fori_loop(0, nw, pick, 0)

    def s2_copy(j):
        return pltpu.make_async_remote_copy(
            st.at[j], rv.at[w], s2_s, s2_r, device_id=(j, n), device_id_type=MESH
        )

    @pl.when(even)
    def _():
        def send(d, _):
            s2_copy((w + d) % nw).start()
            return 0

        lax.fori_loop(1, nw, send, 0)

    @pl.when(jnp.logical_and(holds, jnp.logical_not(even)))
    def _():
        def send(d, _):
            j = (w + d) % nw

            @pl.when((j // NX) % NY == y4)
            def _():
                s2_copy(j).start()

            return 0

        lax.fori_loop(1, nw, send, 0)

    @pl.when(gets)
    def _():
        own = pltpu.make_async_copy(st.at[w], rv.at[w], loc_s)
        own.start()
        own.wait()

    gath_n.ring_b(1)
    gath_1.pair()
    gath_0.pair()
    gath_n.ring_b(2)
    for i in range(8):
        rows = gn[pl.ds(i * 8, 8)].astype(F32).reshape(64, gn.shape[2]).astype(BF16)
        nr[i // 2, i % 2] = rows

    loads["res"].wait()
    partner = yh * 2 + 1 - c
    px[...] = dot_nt(nr[:, 1 - c].reshape(256, nr.shape[3]), res[...]).astype(BF16)
    xcopy = pltpu.make_async_remote_copy(px, pxr, px_s, px_r, device_id=(w, partner), device_id_type=MESH)
    xcopy.start()

    for h in range(4):
        tx[h] = dot_nt(gb[w], nr[h].reshape(128, nr.shape[3])).astype(BF16)
    leads = c == y

    @pl.when(leads)
    def _():
        tr[n] = tx[yh]

    def t_copy(d):
        h = (yh + d) % 4
        return pltpu.make_async_remote_copy(
            tx.at[h], tr.at[n], t_s.at[d], t_r, device_id=(w, h * 2 + y), device_id_type=MESH
        )

    for d in (2, 1, 3):
        t_copy(d).start()

    @pl.when(jnp.logical_not(leads))
    def _():
        t_copy(0).start()

    up, down, far = (yh + 1) % 4, (yh + 3) % 4, (yh + 2) % 4
    @pl.when(gets)
    def _():
        r = rv.at[pl.ds(0, nw - 1)]
        pltpu.make_async_copy(r, r, s2_r).wait()
        right = rv[...].reshape(nw * 16, LANE).T

        @pl.when(even)
        def _():
            at[pl.ds(pl.multiple_of(yh * LANE, LANE), LANE), :] = right

        @pl.when(jnp.logical_not(even))
        def _():
            at[4 * LANE :, :] = right[: at.shape[0] - 4 * LANE]

    def piece(t, half):
        if isinstance(t, int) and t == 4:
            return at.at[pl.ds(t * LANE + half * 48, 48 - half * 16)]
        return at.at[pl.ds(pl.multiple_of(t * LANE + half * 64, 64), 64)]

    def s3(t, half, slot, sem, dest):
        return pltpu.make_async_remote_copy(
            piece(t, half), piece(t, half), s3_s.at[sem], s3_r.at[slot], device_id=(w, dest), device_id_type=MESH
        )

    d4 = (yh - 2 * y + 4) % 4
    even_sends = (
        (yh, 0, 2, 0, up * 2), (yh, 1, 5, 1, down * 2), (yh, 1, 3, 2, up * 2), (yh, 0, 4, 3, down * 2),
        (yh, 0, 0, 4, partner), (yh, 1, 1, 5, partner),
    )
    src_sends = (
        (4, 0, 8, 0, up * 2 + 1), (4, 1, 9, 1, down * 2 + 1), (4, 1, 9, 2, up * 2 + 1), (4, 0, 8, 3, down * 2 + 1),
        (4, 0, 8, 4, partner), (4, 1, 9, 5, partner),
    )

    @pl.when(even)
    def _():
        for args in even_sends:
            s3(*args).start()

    @pl.when(jnp.logical_and(c == 1, d4 == 0))
    def _():
        for args in src_sends:
            s3(*args).start()

    po[...] = dot_nt(nr[:, c].reshape(256, nr.shape[3]), res[...]).reshape(po.shape)
    xcopy.wait_recv()
    for h in range(4):
        po[h] = po[h] + pxr[h * 64 : (h + 1) * 64].astype(F32)
    rsrc[2] = po[far].astype(BF16)

    def far_copy(i, h):
        half = pl.ds(32 * i, 32)
        return pltpu.make_async_remote_copy(
            rsrc.at[2, half], rf.at[i], rr_s.at[2 + i], rf_r.at[i], device_id=(w, h * 2 + c), device_id_type=MESH
        )

    def near_copy(i, h):
        return pltpu.make_async_remote_copy(
            rsrc.at[i], rrcv.at[i], rr_s.at[i], rr_r, device_id=(w, h * 2 + c), device_id_type=MESH
        )

    far_copy(0, up).start()
    far_copy(1, down).start()
    gath_1.direct(1)
    gath_1.direct(2)
    gath_0.direct(1)
    gath_0.direct(2)
    gath_0.direct(3)
    gath_0.direct(4)
    gath_1.ring_b(1)

    @pl.when(leads)
    def _():
        pltpu.make_async_copy(tr.at[pl.ds(0, 7)], tr.at[pl.ds(0, 7)], t_r).wait()
        tsum = tr[0].astype(F32)
        for i in range(1, 8):
            tsum = tsum + tr[i].astype(F32)
        ts[...] = tsum.astype(BF16)
        tg[w] = ts[...]

        def tw_send(d, _):
            pltpu.make_async_remote_copy(
                ts, tg.at[w], tw_s, tw_r, device_id=((w + d) % nw, n), device_id_type=MESH
            ).start()
            return 0

        lax.fori_loop(1, nw, tw_send, 0)

    @pl.when(even)
    def _():
        s3(down, 0, 2, 0, partner).wait_recv()
        s3(down, 0, 6, 6, up * 2).start()
        s3(down, 0, 2, 7, partner).start()
        s3(up, 1, 5, 0, partner).wait_recv()
        s3(up, 1, 7, 8, down * 2).start()
        s3(up, 1, 5, 9, partner).start()

    @pl.when(jnp.logical_and(c == 1, d4 == 1))
    def _():
        s3(4, 0, 8, 0, partner).wait_recv()
        s3(4, 0, 8, 0, up * 2 + 1).start()
        s3(4, 0, 8, 1, partner).start()
        s3(4, 1, 9, 0, partner).wait_recv()
        s3(4, 1, 9, 2, partner).start()

    @pl.when(jnp.logical_and(c == 1, d4 == 3))
    def _():
        s3(4, 1, 9, 0, partner).wait_recv()
        s3(4, 1, 9, 0, down * 2 + 1).start()
        s3(4, 1, 9, 1, partner).start()
        s3(4, 0, 8, 0, partner).wait_recv()
        s3(4, 0, 8, 2, partner).start()

    gath_0.ring_b(1)
    gath_1.ring_b(2)
    far_copy(0, up).wait_recv()
    far_copy(1, down).wait_recv()
    toward = po[up]
    rsrc[0] = jnp.concatenate([toward[:32] + rf[0].astype(F32), toward[32:]], axis=0).astype(BF16)
    near_copy(0, up).start()
    toward = po[down]
    rsrc[1] = jnp.concatenate([toward[:32], toward[32:] + rf[1].astype(F32)], axis=0).astype(BF16)
    near_copy(1, down).start()

    gath_1.ring_b(3)
    @pl.when(even)
    def _():
        s3(down, 1, 3, 0, partner).wait_recv()
        s3(down, 1, 3, 10, partner).start()
        s3(up, 0, 4, 0, partner).wait_recv()
        s3(up, 0, 4, 11, partner).start()

    @pl.when(even)
    def _():
        s3(far, 0, 6, 0, partner).wait_recv()
        s3(far, 0, 6, 12, partner).start()
        s3(far, 1, 7, 0, partner).wait_recv()
        s3(far, 1, 7, 13, partner).start()
        s3(4, 0, 8, 0, partner).wait_recv()
        s3(4, 1, 9, 0, partner).wait_recv()

    @pl.when(jnp.logical_and(c == 1, d4 == 2))
    def _():
        s3(4, 0, 8, 0, partner).wait_recv()
        s3(4, 0, 8, 0, partner).start()
        s3(4, 1, 9, 0, partner).wait_recv()
        s3(4, 1, 9, 1, partner).start()

    def te_copy(i):
        span = pl.ds((i * NY + c) * NX, NX)
        return pltpu.make_async_remote_copy(
            tg.at[span], tg.at[span], te_s, te_r, device_id=(w, partner), device_id_type=MESH
        )

    half_tg = tg.at[pl.ds(0, nw // 2)]

    @pl.when(leads)
    def _():
        r = tg.at[pl.ds(0, nw // 2 - 1)]
        pltpu.make_async_copy(r, r, tw_r).wait()

    @pl.when(jnp.logical_not(leads))
    def _():
        pltpu.make_async_copy(half_tg, half_tg, tw_r).wait()

    for i in range(NZ):
        te_copy(i).start()

    gath_1.ring_b(4)
    gath_0.ring_b(2)
    @pl.when(c == 1)
    def _():
        for t, half, slot in (
            (yh, 0, 0), (yh, 1, 1), (down, 0, 2), (down, 1, 3), (up, 0, 4), (up, 1, 5), (far, 0, 6), (far, 1, 7),
        ):
            s3(t, half, slot, 0, partner).wait_recv()

    fbw = res.shape[0]
    for t in range(res.shape[1] // 256):
        part = slice(t * 256, (t + 1) * 256)
        delta = dot(at[...], gb[:, :, part].reshape(nw * 16, 256))
        mg[:, part] = (res[:, part].astype(F32) + adapter_scale / nw * delta[:fbw]).astype(BF16)

    pltpu.make_async_copy(half_tg, half_tg, te_r).wait()
    term = dot(at[...], tg[...].reshape(nw * 16, LANE))
    tt[...] = term.T.reshape(tt.shape)
    pltpu.make_async_copy(rrcv, rrcv, rr_r).wait()
    acc = po[yh] + rrcv[0].astype(F32) + rrcv[1].astype(F32)
    acc = acc + adapter_scale / nw * tt[c][:, :fbw]
    pj[...] = (acc * inverse_root).astype(BF16)

    @pl.when(jnp.logical_not(holds))
    def _():
        loads["owner"].wait()

    pltpu.make_async_copy(r7, r7, pb_s).wait()
    gath_n.sent()
    gath_0.sent()
    gath_1.sent()
    pltpu.make_async_copy(half_tg, half_tg, te_s).wait()

    @pl.when(leads)
    def _():
        r = tg.at[pl.ds(0, nw - 1)]
        pltpu.make_async_copy(r, r, tw_s).wait()

    @pl.when(jnp.logical_not(leads))
    def _():
        t_copy(0).wait_send()

    for d in (1, 2, 3):
        t_copy(d).wait_send()
    for i, (t, dest) in enumerate(holders):

        @pl.when(n != dest)
        def _():
            s1_copy(i).wait_send()

    @pl.when(even)
    def _():
        r = st.at[pl.ds(0, nw - 1)]
        pltpu.make_async_copy(r, r, s2_s).wait()
        for i in range(14):
            s3(0, 0, 0, i, partner).wait_send()

    @pl.when(jnp.logical_and(holds, jnp.logical_not(even)))
    def _():
        @pl.when(gets)
        def _():
            r = st.at[pl.ds(0, nw // 2 - 1)]
            pltpu.make_async_copy(r, r, s2_s).wait()

        @pl.when(jnp.logical_not(gets))
        def _():
            r = st.at[pl.ds(0, nw // 2)]
            pltpu.make_async_copy(r, r, s2_s).wait()

    for d, halves in ((0, (0, 1, 1, 0, 0, 1)), (1, (0, 0, 1)), (2, (0, 1)), (3, (1, 1, 0))):

        @pl.when(jnp.logical_and(c == 1, d4 == d))
        def _():
            for i, half in enumerate(halves):
                s3(4, half, 0, i, partner).wait_send()

    xcopy.wait_send()
    far_copy(0, up).wait_send()
    far_copy(1, down).wait_send()
    near_copy(0, up).wait_send()
    near_copy(1, down).wait_send()


def per_device(
    activation_cache, token_ids, cotangent, adapter_b, first_b, second_b, adapter_a, first_a, second_a, resident,
    block_owner, next_rows,
):
    dl = activation_cache.shape[2]
    cl = cotangent.shape[2]
    rl, fb = resident.shape
    nw = NZ * NY * NX
    anyspec = pl.BlockSpec(memory_space=pl.ANY)
    dma = pltpu.SemaphoreType.DMA
    vm = pltpu.VMEM
    scratch = [
        vm((1, 128), jnp.int32), pltpu.SMEM((nw,), jnp.int32),
        vm((128, dl), BF16), vm((cl, 128), BF16), vm((16, dl), F32), vm((16, dl), F32), vm((16, dl), F32),
        vm((16, cl), F32), vm((16, cl), F32), vm((16, cl), F32), vm((fb, rl), BF16),
        vm((8, 32, 128), BF16),
        vm((nw, 16, dl), BF16),
        vm((nw, 8, dl), BF16),
        vm((16, 4736), F32),
        vm((5, 8, 16, LANE), BF16),
        vm((nw, 16, LANE), BF16),
        vm((nw, 16, LANE), BF16),
        vm((nw, 16, LANE), BF16),
        vm((4 * LANE + 80, nw * 16), BF16),
        vm((4, 2, 64, dl), BF16),
        vm((256, fb), BF16), vm((256, fb), BF16),
        vm((4, 64, fb), F32),
        vm((3, 64, fb), BF16), vm((2, 64, fb), BF16),
        vm((2, 32, fb), BF16),
        vm((4, 16, LANE), BF16), vm((8, 16, LANE), BF16), vm((16, LANE), BF16), vm((nw, 16, LANE), BF16),
        vm((2, 64, 4 * LANE + 80), F32),
        dma((12,)), dma(()), dma(()),
        dma((13,)), dma((19,)), dma((13,)), dma((3,)),
        dma((4,)), dma(()), dma(()), dma(()), dma(()), dma(()), dma((2,)),
        dma((6,)), dma(()), dma(()), dma(()),
        dma((14,)), dma((10,)),
        dma(()), dma(()), dma((4,)), dma(()), dma(()),
    ]
    merged, projected = pl.pallas_call(
        kernel,
        out_shape=(pltpu.VMEM((fb, rl), BF16), pltpu.VMEM((64, fb), BF16)),
        in_specs=[anyspec] * 12,
        out_specs=(pl.BlockSpec(memory_space=pltpu.VMEM),) * 2,
        scratch_shapes=scratch,
        compiler_params=pltpu.CompilerParams(collective_id=0, has_side_effects=True, vmem_limit_bytes=60 * 1024 * 1024),
        name="merge_step",
    )(
        token_ids, block_owner, activation_cache, jnp.swapaxes(cotangent, 1, 2), adapter_b, first_b, second_b, adapter_a,
        first_a, second_a, resident.T, next_rows,
    )
    return merged.T, projected


def solution(mesh):
    return jax.shard_map(
        per_device,
        mesh=mesh,
        in_specs=(
            P("wide", None, "narrow"),
            P("wide", None),
            P("wide", None, "narrow"),
            P("wide", None, "narrow"),
            P("wide", None, "narrow"),
            P("wide", None, "narrow"),
            P("wide", None, "narrow"),
            P("wide", None, "narrow"),
            P("wide", None, "narrow"),
            P("narrow", "wide"),
            P(),
            P("wide", "narrow"),
        ),
        out_specs=(P("narrow", "wide"), P("narrow", "wide")),
        check_vma=False,
    )
```
